256 devices in a mesh: row: 16 (over x_lo, z), col: 16 (over y, x_hi, core).
Axes of the slice: x: 4 (x_hi: 2, x_lo: 2; x = x_hi * 2 + x_lo), y: 4, z: 8, core: 2. Of those that a mesh axis runs over, the one named last changes fastest.
Arguments:
- queries: bfloat16 [65536, 2048], P(('row', 'col')), may hold values from -200 to 200
- keys: bfloat16 [65536, 512], P(('row', 'col')), may hold values from -6 to 6
- values: bfloat16 [65536, 512], P(('row', 'col')), may hold values from -6 to 6
- mid_key_weight: bfloat16 [1024, 128], replicated, may hold values from -0.1875 to 0.1875
- mid_value_weight: bfloat16 [1024, 128], replicated, may hold values from -0.1875 to 0.1875
- far_key_weight: bfloat16 [2048, 128], replicated, may hold values from -0.125 to 0.125
- far_value_weight: bfloat16 [2048, 128], replicated, may hold values from -0.125 to 0.125
Outputs:
- attended: bfloat16 [65536, 2048], P(('row', 'col'))
The draws below stay inside these ranges and needn't reach their ends.
All inputs are finite; a program needn't handle non-finite values.
Results may differ from the reference program's by a relative error of at most 0.012.
Values may be sent and summed in bfloat16 or wider, within the bound.
No kernel may reach another device: no remote copies, remote signals or barrier semaphores. Data moves between devices by JAX's collectives and lax.ppermute only.
A program may use at most 128 MiB of HBM per device.

```python
import jax
import jax.numpy as jnp
from jax import lax

HQ = 16
HK = 4
DH = 128
BLOCK = 512
MID = 8
FAR = 16
TOK_DEV = 256
TOKENS = 65536
N_ROW = 16
N_COL = 16
DEVICES = 256


def draw_queries(key, part):
    key_one = jax.random.fold_in(key, 0)
    normal_part = jnp.clip(jax.random.normal(key_one, (TOKENS, HQ * DH), jnp.float32), -6.0, 6.0)
    return (1.5 * normal_part).astype(jnp.bfloat16)


def block_levels(own_key, extent, cuts, low, largest):
    factor_of, own = 1.0, jax.random.fold_in(own_key, 6)
    for axis_at, shards_of in cuts:
        heights = jnp.exp(jax.random.uniform(jax.random.fold_in(own, axis_at), (shards_of,), jnp.float32, low / len(cuts), largest / len(cuts)))
        factor_of = factor_of * jnp.repeat(heights, extent[axis_at] // shards_of).reshape([-1 if axis == axis_at else 1 for axis in range(len(extent))])
    return factor_of


def centred(own_key, shape, spread, most, cuts=(), kind=jnp.bfloat16):
    entries = spread * jax.random.normal(own_key, shape, jnp.float32)
    if cuts:
        entries = entries * block_levels(own_key, shape, cuts, -0.22, 0.18)
    return jnp.clip(entries, -most, most).astype(kind)


def setup_inputs(seed: int = 0) -> dict:
    splits = jax.random.split(jax.random.key(seed), 8)
    return {
        "queries": draw_queries(jax.random.fold_in(splits[7], 71), 0),
        "keys": centred(splits[1], (TOKENS, HK * DH), 1.0, 6.0, ((0, 256),)),
        "values": centred(splits[2], (TOKENS, HK * DH), 1.0, 6.0, ((0, 256),)),
        "mid_key_weight": centred(splits[3], (MID * DH, DH), (MID * DH) ** -0.5, 0.1875),
        "mid_value_weight": centred(splits[4], (MID * DH, DH), (MID * DH) ** -0.5, 0.1875),
        "far_key_weight": centred(splits[5], (FAR * DH, DH), (FAR * DH) ** -0.5, 0.125),
        "far_value_weight": centred(splits[6], (FAR * DH, DH), (FAR * DH) ** -0.5, 0.125),
    }


NEG_FILL = -1e30


def squeeze_groups(source, weight, squeeze):
    group_count = source.shape[0] // squeeze
    grouped = source.reshape(group_count, squeeze, HK, DH).transpose(0, 2, 1, 3).reshape(group_count, HK, squeeze * DH)
    merged = jnp.einsum("nhr,rd->nhd", grouped.astype(jnp.float32), weight.astype(jnp.float32))
    return merged.astype(jnp.bfloat16).reshape(group_count, HK * DH)


def attend(queries, keys, values, visible):
    group_size = HQ // HK
    query_rows = queries.shape[0]
    query4 = queries.reshape(query_rows, HK, group_size, DH).astype(jnp.float32)
    key_heads = keys.reshape(keys.shape[0], HK, DH).astype(jnp.float32)
    value_heads = values.reshape(values.shape[0], HK, DH).astype(jnp.float32)
    scores = jnp.einsum("thgd,shd->hgts", query4, key_heads) * (DH ** -0.5)
    top_score = jnp.max(jnp.where(visible, scores, NEG_FILL), axis=-1, keepdims=True)
    weights = jnp.exp(jnp.where(visible, scores - top_score, NEG_FILL))
    weight_sum = jnp.sum(weights, axis=-1)
    rounded = lax.optimization_barrier(weights.astype(jnp.bfloat16))
    mixed_out = jnp.einsum("hgts,shd->thgd", rounded.astype(jnp.float32), value_heads)
    weight_sum = jnp.transpose(weight_sum, (2, 0, 1))[..., None]
    return (mixed_out / jnp.maximum(weight_sum, 1.0)).reshape(query_rows, HQ * DH)


def reference(queries, keys, values, mid_key_weight, mid_value_weight, far_key_weight, far_value_weight):
    tok_rows = TOK_DEV
    mid_keys = squeeze_groups(keys, mid_key_weight, MID)
    mid_values = squeeze_groups(values, mid_value_weight, MID)
    far_keys = squeeze_groups(keys, far_key_weight, FAR)
    far_values = squeeze_groups(values, far_value_weight, FAR)
    row_mid = N_COL * tok_rows // MID
    row_far = N_COL * tok_rows // FAR
    zero_rows = jnp.zeros((3 * tok_rows, HK * DH), keys.dtype)
    padded_keys = jnp.concatenate([zero_rows, keys], axis=0)
    padded_values = jnp.concatenate([zero_rows, values], axis=0)
    far_row = jnp.arange(N_ROW * row_far, dtype=jnp.int32) // row_far

    def one_tile(device_pos):
        first_pos = device_pos * tok_rows
        query_pos = first_pos + jnp.arange(tok_rows, dtype=jnp.int32)
        query_tile = lax.dynamic_slice_in_dim(queries, first_pos, tok_rows, 0)
        near_keys = lax.dynamic_slice_in_dim(padded_keys, first_pos, 4 * tok_rows, 0)
        near_values = lax.dynamic_slice_in_dim(padded_values, first_pos, 4 * tok_rows, 0)
        key_pos = first_pos - 3 * tok_rows + jnp.arange(4 * tok_rows, dtype=jnp.int32)
        near_seen = (key_pos[None, :] <= query_pos[:, None]) & (key_pos[None, :] >= 0) & (key_pos[None, :] // BLOCK >= query_pos[:, None] // BLOCK - 1)
        grid_row = device_pos // N_COL
        row_first = grid_row * (N_COL * tok_rows)
        mid_k = lax.dynamic_slice_in_dim(mid_keys, grid_row * row_mid, row_mid, 0)
        mid_v = lax.dynamic_slice_in_dim(mid_values, grid_row * row_mid, row_mid, 0)
        mid_end = row_first + MID * jnp.arange(row_mid, dtype=jnp.int32) + MID - 1
        mid_seen = mid_end[None, :] <= query_pos[:, None]
        far_seen = jnp.broadcast_to(far_row[None, :] < grid_row, (tok_rows, N_ROW * row_far))
        summed = attend(query_tile, near_keys, near_values, near_seen)
        summed = summed + attend(query_tile, mid_k, mid_v, mid_seen)
        summed = summed + attend(query_tile, far_keys, far_values, far_seen)
        return summed.astype(jnp.bfloat16)

    all_tiles = lax.map(one_tile, jnp.arange(DEVICES, dtype=jnp.int32))
    return all_tiles.reshape(DEVICES * tok_rows, HQ * DH)
```

```python
import functools

import jax
import jax.numpy as jnp
import numpy as np
from jax import lax
from jax.experimental import pallas as pl
from jax.experimental.pallas import tpu as pltpu
from jax.sharding import PartitionSpec as P

HQ = 16
HK = 4
DH = 128
BLOCK = 512
MID = 8
FAR = 16
TOK = 256
CHIP = 2 * TOK
HEADS = HQ // 2
NEG = -1e30
EXP2_SCALE = float(DH**-0.5 * np.log2(np.e))
BF16 = jnp.bfloat16
F32 = jnp.float32
NT = (((1,), (1,)), ((), ()))
N_X, N_Y, N_Z = 4, 4, 8
AXES = ("row", "col")


def place(d):
    row, col = d // 16, d % 16
    return (col // 2 % 2) * 2 + row // N_Z, col // 4, row % N_Z, col % 2


def device(x, y, z, core):
    return ((x % 2) * N_Z + z) * 16 + (y * 2 + x // 2) * 2 + core


def shift(v, axis, by, wrap=True, from_even=False):
    pairs = []
    for d in range(256):
        at = list(place(d))
        if from_even and at[0] % 2:
            continue
        size = (N_X, N_Y, N_Z)[axis]
        to = at[axis] + by
        if not wrap and not 0 <= to < size:
            continue
        at[axis] = to % size
        pairs.append((d, device(*at)))
    return lax.ppermute(v, AXES, pairs)


def other_core(v):
    return lax.ppermute(v, AXES, [(d, d ^ 1) for d in range(256)])


def next_chip(v):
    return lax.ppermute(v, AXES, [(d, d + 2) for d in range(254)])


def squeeze_kernel(s_ref, k_ref, v_ref, got_ref, mk_ref, mv_ref, fk_ref, fv_ref, chip_ref, mid_ref, far_ref, x_ref):
    core = s_ref[0]
    for i, (own_ref, m_ref, f_ref) in enumerate(((k_ref, mk_ref, fk_ref), (v_ref, mv_ref, fv_ref))):
        for h in range(2):
            lanes = slice(h * DH, (h + 1) * DH)
            own = own_ref[:, lanes].astype(F32)
            got = got_ref[i, :, lanes].astype(F32)
            x_ref[pl.ds(pl.multiple_of(h * CHIP + core * TOK, TOK), TOK), :] = own
            x_ref[pl.ds(pl.multiple_of(h * CHIP + (1 - core) * TOK, TOK), TOK), :] = got
            chip_ref[i, :, lanes] = x_ref[h * CHIP : (h + 1) * CHIP, :].astype(BF16)
        for run, w_ref in ((MID, m_ref), (FAR, f_ref)):
            rows = 2 * CHIP // run
            laid = jnp.concatenate(
                [x_ref[pl.ds(j, rows, stride=run), :].astype(BF16) for j in range(run)], axis=1
            )
            merged = jnp.dot(laid, w_ref[...], preferred_element_type=F32).astype(BF16)
            half = rows // 2
            for h in range(2):
                part = merged[h * half : (h + 1) * half]
                if run == MID:
                    mid_ref[0, i, :, h * DH : (h + 1) * DH] = part
                else:
                    far_ref[h, 0, i] = part


def squeeze(scalars, k_own, v_own, got, mk, mv, fk, fv):
    whole = lambda shape: pl.BlockSpec(shape, lambda i, s: (0,) * len(shape))
    return pl.pallas_call(
        squeeze_kernel,
        grid_spec=pltpu.PrefetchScalarGridSpec(
            num_scalar_prefetch=1,
            grid=(1,),
            in_specs=[
                pl.BlockSpec((TOK, 2 * DH), lambda i, s: (0, s[0])),
                pl.BlockSpec((TOK, 2 * DH), lambda i, s: (0, s[0])),
                whole((2, TOK, 2 * DH)),
                whole((MID * DH, DH)),
                whole((MID * DH, DH)),
                whole((FAR * DH, DH)),
                whole((FAR * DH, DH)),
            ],
            out_specs=[
                whole((2, CHIP, 2 * DH)),
                whole((1, 2, CHIP // MID, 2 * DH)),
                whole((2, 1, 2, CHIP // FAR, DH)),
            ],
            scratch_shapes=[pltpu.VMEM((2 * CHIP, DH), F32)],
        ),
        out_shape=[
            jax.ShapeDtypeStruct((2, CHIP, 2 * DH), BF16),
            jax.ShapeDtypeStruct((1, 2, CHIP // MID, 2 * DH), BF16),
            jax.ShapeDtypeStruct((2, 1, 2, CHIP // FAR, DH), BF16),
        ],
        name="squeeze",
        compiler_params=pltpu.CompilerParams(vmem_limit_bytes=16 << 20),
        cost_estimate=pl.CostEstimate(flops=4 * 10**8, bytes_accessed=3 << 20, transcendentals=0),
    )(scalars, k_own, v_own, got, mk, mv, fk, fv)


def step(q, k, v, fix, state):
    s = lax.dot_general(q, k, NT, preferred_element_type=F32)
    if fix is not None:
        s = fix(s)
    top = jnp.max(s, axis=1, keepdims=True)
    if state is not None:
        top = jnp.maximum(top, state[0])
    p = jnp.exp2((s - top) * EXP2_SCALE).astype(BF16)
    v = jnp.concatenate([v, jnp.ones(v.shape, BF16)], axis=1)
    got = jnp.dot(p, v, preferred_element_type=F32)
    if state is not None:
        got = got + state[1] * jnp.exp2((state[0] - top) * EXP2_SCALE)
    return top, got


def load_state(o_ref, stat_ref, t, h):
    stat = stat_ref[t]
    lane = lax.broadcasted_iota(jnp.int32, stat.shape, 1)
    top = jnp.sum(jnp.where(lane == h, stat, 0.0), axis=1, keepdims=True)
    total = jnp.sum(jnp.where(lane == HEADS + h, stat, 0.0), axis=1, keepdims=True)
    return top, jnp.concatenate([o_ref[t], jnp.broadcast_to(total, stat.shape)], axis=1)


def save_state(o_ref, stat_ref, t, h, state):
    top, got = state
    o_ref[t] = got[:, :DH]
    lane = lax.broadcasted_iota(jnp.int32, (TOK, DH), 1)
    old = jnp.where(h == 0, 0.0, stat_ref[t])
    stat_ref[t] = jnp.where(lane == h, top, jnp.where(lane == HEADS + h, got[:, DH:], old))


def finish(state):
    top, got = state
    return jnp.where(top > 0.5 * NEG, got[:, :DH] / jnp.maximum(got[:, DH:], 1.0), 0.0)


def own_kernel(s_ref, qa_ref, qb_ref, kv_ref, o_ref, stat_ref):
    h = pl.program_id(0)
    core = s_ref[0]
    for t, q_ref in enumerate((qa_ref, qb_ref)):
        base = core * TOK if t == 0 else (1 - core) * TOK
        q, state = q_ref[...], None
        for c in range(2):
            keys = slice(c * TOK, (c + 1) * TOK)

            def causal(s, c=c):
                row = lax.broadcasted_iota(jnp.int32, s.shape, 0) + base
                col = lax.broadcasted_iota(jnp.int32, s.shape, 1) + c * TOK
                return jnp.where(col <= row, s, NEG)

            state = step(q, kv_ref[0, keys], kv_ref[1, keys], causal, state)
        save_state(o_ref, stat_ref, t, h, state)


def near_mid_kernel(s_ref, qa_ref, qb_ref, kv_ref, m0_ref, m1_ref, m2_ref, m3_ref, tab_ref, o_in, stat_in, out_ref):
    h = pl.program_id(0)
    core = s_ref[0]
    hidden = jnp.where(s_ref[1] > 0, 0.0, NEG)
    mids = (m0_ref, m1_ref, m2_ref, m3_ref)
    mid_k = jnp.concatenate([m[:, 0].reshape(-1, DH) for m in mids], axis=0)
    mid_v = jnp.concatenate([m[:, 1].reshape(-1, DH) for m in mids], axis=0)
    ends = tab_ref[3:4, : mid_k.shape[0]]
    for t, q_ref in enumerate((qa_ref, qb_ref)):
        base = core * TOK if t == 0 else (1 - core) * TOK
        q = q_ref[...]
        near = step(q, kv_ref[0], kv_ref[1], lambda s: s + hidden, load_state(o_in, stat_in, t, h))

        def ended(s):
            row = lax.broadcasted_iota(jnp.int32, s.shape, 0) + base
            return jnp.where(ends <= row.astype(F32), s, NEG)

        mid = step(q, mid_k, mid_v, ended, None)
        out_ref[t] = finish(near) + finish(mid)


def far_kernel(parts, first, last, *refs):
    s_ref, qa_ref, qb_ref = refs[:3]
    part_refs, refs = refs[3 : 3 + 2 * len(parts)], refs[3 + 2 * len(parts) :]
    tab_ref, refs = refs[0], refs[1:]
    if not first:
        o_in, stat_in, refs = refs[0], refs[1], refs[2:]
    if last:
        sum_ref, keep_ref, send_ref = refs
    else:
        o_ref, stat_ref = refs
    h = pl.program_id(0)

    def run(half):
        for t, q_ref in enumerate((qa_ref, qb_ref)):
            q = q_ref[...]
            state = None if first else load_state(o_in, stat_in, t, h)
            for i, rows in enumerate(parts):
                ref = part_refs[2 * i + half]
                n = ref.shape[0] // 2
                for c in range(2):
                    pieces = slice(c * n, (c + 1) * n)
                    k = ref[pieces, 0].reshape(-1, DH)
                    v = ref[pieces, 1].reshape(-1, DH)
                    width = k.shape[0]
                    bias = tab_ref[rows[half] : rows[half] + 1, c * width : (c + 1) * width]
                    state = step(q, k, v, lambda s, bias=bias: s + bias, state)
            if last:
                (keep_ref, send_ref)[t][...] = (finish(state) + sum_ref[t]).astype(BF16)
            else:
                save_state(o_ref, stat_ref, t, h, state)

    @pl.when(h < HEADS // 2)
    def _():
        run(0)

    @pl.when(h >= HEADS // 2)
    def _():
        run(1)


Q_SPECS = [
    pl.BlockSpec((TOK, DH), lambda h, s: (0, s[0] * HEADS + h)),
    pl.BlockSpec((TOK, DH), lambda h, s: (0, h)),
]
KV_SPEC = pl.BlockSpec((2, CHIP, DH), lambda h, s: (0, 0, h // 2 // 2))
MID_SPEC = pl.BlockSpec((2, 2, CHIP // MID, DH), lambda h, s: (0, 0, 0, h // 4))
O_SPEC = pl.BlockSpec((2, TOK, DH), lambda h, s: (0, 0, h))
STAT_SPEC = pl.BlockSpec((2, TOK, DH), lambda h, s: (0, 0, 0))
TAB_SPEC = pl.BlockSpec((8, 1024), lambda h, s: (0, 0))
HALF_SPEC = pl.BlockSpec((TOK, DH), lambda h, s: (0, h))
O_SHAPE = jax.ShapeDtypeStruct((2, TOK, HEADS * DH), F32)
STAT_SHAPE = jax.ShapeDtypeStruct((2, TOK, DH), F32)
HALF_SHAPE = jax.ShapeDtypeStruct((TOK, HEADS * DH), BF16)


def call(kernel, name, keys, in_specs, out_specs, out_shape, *args):
    rows = CHIP * HEADS
    return pl.pallas_call(
        kernel,
        grid_spec=pltpu.PrefetchScalarGridSpec(
            num_scalar_prefetch=1, grid=(HEADS,), in_specs=in_specs, out_specs=out_specs
        ),
        out_shape=out_shape,
        name=name,
        compiler_params=pltpu.CompilerParams(vmem_limit_bytes=24 << 20),
        cost_estimate=pl.CostEstimate(
            flops=6 * rows * keys * DH, bytes_accessed=6 << 20, transcendentals=rows * keys
        ),
    )(*args)


def far_call(name, parts, chunks, scalars, qa, qb, tab, state=None, total=None):
    in_specs = list(Q_SPECS)
    args = [scalars, qa, qb]
    for a, b in chunks:
        for v in (a, b):
            in_specs.append(pl.BlockSpec(v.shape, lambda h, s: (0, 0, 0, 0)))
            args.append(v)
    in_specs.append(TAB_SPEC)
    args.append(tab)
    if state is not None:
        in_specs += [O_SPEC, STAT_SPEC]
        args += list(state)
    if total is not None:
        in_specs.append(O_SPEC)
        args.append(total)
        outs = [HALF_SPEC, HALF_SPEC], [HALF_SHAPE, HALF_SHAPE]
    else:
        outs = [O_SPEC, STAT_SPEC], [O_SHAPE, STAT_SHAPE]
    kernel = functools.partial(far_kernel, parts, state is None, total is not None)
    return call(kernel, name, 1024 * len(parts), in_specs, *outs, *args)


def tables(row, x, z, chip_row):
    z_at = np.array([0, 4, -1, 3, 1, 5, -2, 2])
    piece_z = jnp.asarray(np.tile(np.repeat(z_at, CHIP // FAR), 4), jnp.int32)
    piece_x = jnp.asarray(np.repeat(np.array([0, -1, 1, -2]), 8 * CHIP // FAR), jnp.int32)
    src_z = (z + piece_z) % N_Z
    rows_a = ((x + piece_x) % 2) * N_Z + src_z
    rows_same = (x % 2) * N_Z + src_z
    rows_other = ((x + 1) % 2) * N_Z + src_z
    bias = jnp.where(jnp.stack([rows_a, rows_same, rows_other]) < row, 0.0, NEG).astype(F32)
    y, x_hi = chip_row // 2, chip_row % 2
    back = jnp.asarray(np.repeat(np.arange(4), 128), jnp.int32)
    flip = jnp.asarray(np.tile(np.repeat(np.arange(2), 64), 4), jnp.int32)
    run = jnp.asarray(np.tile(np.arange(64), 8), jnp.int32)
    src = (y - back) * 2 + jnp.where(flip == 1, 1 - x_hi, x_hi)
    ends = ((src - chip_row) * CHIP + run * MID + MID - 1).astype(F32)
    ends = jnp.where(back > y, 1e9, ends)
    ends = jnp.concatenate([ends, jnp.full((512,), 1e9, F32)])
    return jnp.concatenate([bias, ends[None], jnp.zeros((4, 1024), F32)])


def body(queries, keys, values, mk, mv, fk, fv):
    row, col = lax.axis_index("row"), lax.axis_index("col")
    core, chip_row = col % 2, col // 2
    x, z = (chip_row % 2) * 2 + row // N_Z, row % N_Z
    scalars = jnp.stack([core, row * 8 + chip_row]).astype(jnp.int32)
    tab = tables(row, x, z, chip_row)

    def for_other(a):
        half = a.shape[1] // 2
        return jnp.where(core == 0, a[:, half:], a[:, :half])

    got = other_core(jnp.stack([for_other(keys), for_other(values)]))
    q_got = other_core(for_other(queries))
    chip_kv, mid, far = squeeze(scalars, keys, values, got, mk, mv, fk, fv)

    far = jnp.concatenate([far, shift(far, 2, 4)], axis=1)
    far = jnp.concatenate([far, shift(far, 2, 1), shift(far, 2, -1), shift(far, 2, 2)], axis=1)
    prev_kv = next_chip(chip_kv)
    mid = jnp.concatenate([mid, shift(mid, 0, 2)], axis=0)
    mids = [mid] + [shift(mid, 1, d, wrap=False) for d in (1, 2, 3)]
    a, b = far[0], far[1]
    a = jnp.concatenate(
        [a, shift(a, 0, 1, from_even=True), shift(a, 0, -1, from_even=True), shift(a, 0, 2)], axis=0
    )
    b = jnp.concatenate([b, shift(b, 1, 1), shift(b, 1, -1), shift(b, 1, 2)], axis=0)
    a1, b1 = shift(a, 1, 1), shift(b, 0, 1, from_even=True)
    a2, b2 = shift(a, 1, -1), shift(b, 0, -1, from_even=True)
    a3, b3 = shift(a, 1, 2), shift(b, 0, 2)

    near = call(
        own_kernel, "near_own", 512, Q_SPECS + [KV_SPEC], [O_SPEC, STAT_SPEC], [O_SHAPE, STAT_SHAPE],
        scalars, queries, q_got, chip_kv,
    )
    total = call(
        near_mid_kernel, "near_mid", 1024,
        Q_SPECS + [KV_SPEC] + [MID_SPEC] * 4 + [TAB_SPEC, O_SPEC, STAT_SPEC], O_SPEC, O_SHAPE,
        scalars, queries, q_got, prev_kv, *mids, tab, *near,
    )
    state = far_call("far_0", [(0, 1)], [(a, b)], scalars, queries, q_got, tab)
    state = far_call("far_1", [(0, 2), (0, 2)], [(a1, b1), (a2, b2)], scalars, queries, q_got, tab, state)
    keep, send = far_call("far_2", [(0, 1)], [(a3, b3)], scalars, queries, q_got, tab, state, total)
    back = other_core(send)
    return jnp.concatenate([jnp.where(core == 0, keep, back), jnp.where(core == 0, back, keep)], axis=1)


def solution(mesh):
    split = P(("row", "col"), None)
    return jax.shard_map(
        body,
        mesh=mesh,
        in_specs=(split, split, split, P(), P(), P(), P()),
        out_specs=split,
        check_vma=False,
    )
```

```python
import functools

import jax
import jax.numpy as jnp
import numpy as np
from jax import lax
from jax.experimental import pallas as pl
from jax.experimental.pallas import tpu as pltpu
from jax.sharding import PartitionSpec as P

HQ = 16
HK = 4
DH = 128
BLOCK = 512
MID = 8
FAR = 16
TOK = 256
CHIP = 2 * TOK
HEADS = HQ // 2
NEG = -1e30
EXP2_SCALE = float(DH**-0.5 * np.log2(np.e))
BF16 = jnp.bfloat16
F32 = jnp.float32
NT = (((1,), (1,)), ((), ()))
N_X, N_Y, N_Z = 4, 4, 8
X, Y, Z = 0, 1, 2
PACK_VMEM = 16 << 20
AXES = ("row", "col")


def place(d):
    row, col = d // 16, d % 16
    return (col // 2 % 2) * 2 + row // N_Z, col // 4, row % N_Z, col % 2


def device(x, y, z, core):
    return ((x % 2) * N_Z + z) * 16 + (y * 2 + x // 2) * 2 + core


def route(move):
    pairs = [(d, move(*place(d))) for d in range(256)]
    return [(d, device(*to)) for d, to in pairs if to is not None]


def moved(at, axis, by):
    to = list(at)
    to[axis] = (to[axis] + by) % (N_X, N_Y, N_Z)[axis]
    return to


def hop(v, axis, by):
    return lax.ppermute(v, AXES, route(lambda *at: moved(at, axis, by)))


def swap_y(v, bit):
    return lax.ppermute(v, AXES, route(lambda x, y, z, core: (x, y ^ bit, z, core)))


def plane_hop(v, first, by):
    axes = (first, X + Y - first)

    def move(*at):
        axis = axes[at[3]]
        if axis == X and by % 2 and at[X] % 2:
            return None
        return moved(at, axis, by)

    return lax.ppermute(v, AXES, route(move))


def other_core(v):
    return lax.ppermute(v, AXES, [(d, d ^ 1) for d in range(256)])


def next_chip(v):
    return lax.ppermute(v, AXES, [(d, d + 2) for d in range(254)])


VMEM = pl.BlockSpec(memory_space=pltpu.VMEM)
HBM = pl.BlockSpec(memory_space=pltpu.HBM)
STATE = [jax.ShapeDtypeStruct((2, TOK, HEADS * DH), F32)] * 3
HALF = jax.ShapeDtypeStruct((TOK, HEADS * DH), BF16)


def where_am_i():
    row, col = lax.axis_index("row"), lax.axis_index("col")
    return row, col // 2, col % 2


def own_half(core, width):
    return pl.ds(pl.multiple_of(core * width, width), width)


def copy_all(pairs, sems):
    copies = [pltpu.make_async_copy(src, dst, sems.at[i]) for i, (src, dst) in enumerate(pairs)]
    for copy in copies:
        copy.start()
    return copies


def tables(row, chip, core):
    lane = lax.broadcasted_iota(jnp.int32, (1, 1024), 1)

    def back(i):
        return jnp.where(i == 0, 0, jnp.where(i == 1, -1, jnp.where(i == 2, 1, -2)))

    y, x_hi = chip // 2, chip % 2
    x_lo, z = row // N_Z, row % N_Z
    src_z = (z + back((lane >> 6) & 3) + 4 * ((lane >> 5) & 1) + N_Z) & (N_Z - 1)
    line = jnp.where(core == 0, (x_lo + back(lane >> 8)) & 1, x_lo)
    other = jnp.where(core == 0, line, 1 - x_lo)
    coarse = [jnp.where(x * N_Z + src_z < row, 0.0, NEG) for x in (line, other)]
    src_y = y ^ ((lane >> 7) & 3)
    src = src_y * 2 + jnp.where((lane >> 6) & 1 == 1, 1 - x_hi, x_hi)
    ends = (src - chip) * CHIP + (lane & 63) * MID + MID - 1
    return coarse + [ends.astype(F32)]


def pack_kernel(q_ref, k_ref, v_ref, w0, w1, w2, w3, kv_out, q_out, kv_own, q_own, x0, x1, x2, x3, tab_ref, sems):
    row, chip, core = where_am_i()
    mine, theirs = (own_half(c, 2 * DH) for c in (core, 1 - core))
    copies = copy_all(
        [(k_ref.at[:, theirs], kv_out.at[0]), (v_ref.at[:, theirs], kv_out.at[1]),
         (k_ref.at[:, mine], kv_own.at[0]), (v_ref.at[:, mine], kv_own.at[1]),
         (q_ref.at[:, own_half(1 - core, HEADS * DH)], q_out),
         (w0, x0), (w1, x1), (w2, x2), (w3, x3),
         (q_ref.at[:, own_half(core, HEADS * DH)], q_own)],
        sems,
    )
    for i, line in enumerate(tables(row, chip, core)):
        tab_ref[i : i + 1, :] = line
    for copy in copies:
        copy.wait()


def pack(q, k, v, *weights):
    kv = jax.ShapeDtypeStruct((2, TOK, 2 * DH), BF16)
    return pl.pallas_call(
        pack_kernel,
        in_specs=[HBM] * 7,
        out_specs=[VMEM] * 9,
        out_shape=[kv, HALF, kv, HALF]
        + [jax.ShapeDtypeStruct(w.shape, BF16) for w in weights]
        + [jax.ShapeDtypeStruct((8, 1024), F32)],
        scratch_shapes=[pltpu.SemaphoreType.DMA((10,))],
        name="pack",
        compiler_params=pltpu.CompilerParams(vmem_limit_bytes=PACK_VMEM),
        cost_estimate=pl.CostEstimate(flops=0, bytes_accessed=3 << 20, transcendentals=0),
    )(*(pltpu.with_memory_space_constraint(a, pltpu.HBM) for a in (q, k, v, *weights)))


def unpack_kernel(keep_ref, back_ref, out_ref, sems):
    core = where_am_i()[2]
    for copy in copy_all(
        [(keep_ref, out_ref.at[:, own_half(core, HEADS * DH)]),
         (back_ref, out_ref.at[:, own_half(1 - core, HEADS * DH)])],
        sems,
    ):
        copy.wait()


def unpack(keep, back):
    return pl.pallas_call(
        unpack_kernel,
        in_specs=[VMEM] * 2,
        out_specs=HBM,
        out_shape=jax.ShapeDtypeStruct((TOK, HQ * DH), BF16),
        scratch_shapes=[pltpu.SemaphoreType.DMA((2,))],
        name="unpack",
        compiler_params=pltpu.CompilerParams(vmem_limit_bytes=16 << 20),
        cost_estimate=pl.CostEstimate(flops=0, bytes_accessed=2 << 20, transcendentals=0),
    )(keep, back)


def join_kernel(*refs):
    at = 0
    for ref in refs[:-1]:
        refs[-1][at : at + ref.shape[0]] = ref[...]
        at += ref.shape[0]


def join(*parts):
    rows = sum(part.shape[0] for part in parts)
    return pl.pallas_call(
        join_kernel,
        in_specs=[VMEM] * len(parts),
        out_specs=VMEM,
        out_shape=jax.ShapeDtypeStruct((rows, *parts[0].shape[1:]), BF16),
        name="join",
        compiler_params=pltpu.CompilerParams(vmem_limit_bytes=8 << 20),
        cost_estimate=pl.CostEstimate(flops=0, bytes_accessed=1 << 20, transcendentals=0),
    )(*parts)


def squeeze_kernel(own_ref, got_ref, mk_ref, mv_ref, fk_ref, fv_ref, chip_ref, mid_ref, far_ref, x_ref):
    core = where_am_i()[2]
    for i, (m_ref, f_ref) in enumerate(((mk_ref, fk_ref), (mv_ref, fv_ref))):
        for h in range(2):
            lanes = slice(h * DH, (h + 1) * DH)
            for ref, c in ((own_ref, core), (got_ref, 1 - core)):
                at = pl.ds(pl.multiple_of(h * CHIP + c * TOK, TOK), TOK)
                x_ref[at, :] = ref[i, :, lanes].astype(F32)
            chip_ref[i, :, lanes] = x_ref[h * CHIP : (h + 1) * CHIP, :].astype(BF16)
        for run, w_ref in ((MID, m_ref), (FAR, f_ref)):
            rows = 2 * CHIP // run
            laid = jnp.concatenate(
                [x_ref[pl.ds(j, rows, stride=run), :].astype(BF16) for j in range(run)], axis=1
            )
            merged = jnp.dot(laid, w_ref[...], preferred_element_type=F32).astype(BF16)
            half = rows // 2
            for h in range(2):
                part = merged[h * half : (h + 1) * half]
                if run == MID:
                    mid_ref[0, i, :, h * DH : (h + 1) * DH] = part
                else:
                    far_ref[0, h, i] = part


def squeeze(own, got, mk, mv, fk, fv):
    return pl.pallas_call(
        squeeze_kernel,
        in_specs=[VMEM] * 6,
        out_specs=[VMEM] * 3,
        scratch_shapes=[pltpu.VMEM((2 * CHIP, DH), F32)],
        out_shape=[
            jax.ShapeDtypeStruct((2, CHIP, 2 * DH), BF16),
            jax.ShapeDtypeStruct((1, 2, CHIP // MID, 2 * DH), BF16),
            jax.ShapeDtypeStruct((1, 2, 2, CHIP // FAR, DH), BF16),
        ],
        name="squeeze",
        compiler_params=pltpu.CompilerParams(vmem_limit_bytes=16 << 20),
        cost_estimate=pl.CostEstimate(flops=4 * 10**8, bytes_accessed=3 << 20, transcendentals=0),
    )(own, got, mk, mv, fk, fv)


def spread(x, lanes):
    return jnp.concatenate([x] * (lanes // DH), axis=1)


def step(q, k, v, fix, state):
    s = fix(lax.dot_general(q, k, NT, preferred_element_type=F32))
    top = jnp.broadcast_to(jnp.max(s, axis=1, keepdims=True), (s.shape[0], DH))
    if state is not None:
        top = jnp.maximum(top, state[0])
    p = jnp.exp2((s - spread(top, s.shape[1])) * EXP2_SCALE).astype(BF16)
    v = jnp.concatenate([v, jnp.ones(v.shape, BF16)], axis=1)
    got = jnp.dot(p, v, preferred_element_type=F32)
    if state is not None:
        got = got + state[1] * spread(jnp.exp2((state[0] - top) * EXP2_SCALE), 2 * DH)
    return top, got


def load_state(refs, t, lanes):
    o, l, m = (ref[t, :, lanes] for ref in refs)
    return m, jnp.concatenate([o, l], axis=1)


def save_state(refs, t, lanes, state):
    refs[0][t, :, lanes] = state[1][:, :DH]
    refs[1][t, :, lanes] = state[1][:, DH:]
    refs[2][t, :, lanes] = state[0]


def finish(state):
    top, got = state
    return jnp.where(top > 0.5 * NEG, got[:, :DH] / jnp.maximum(got[:, DH:], 1.0), 0.0)


def tiles(q_refs):
    for h in range(HEADS):
        lanes = slice(h * DH, (h + 1) * DH)
        for t in range(2):
            yield h // 4, lanes, t, q_refs[t][:, lanes]


def row_of(t, core, shape):
    return lax.broadcasted_iota(jnp.int32, shape, 0) + (core if t == 0 else 1 - core) * TOK


def own_kernel(qa_ref, qb_ref, kv_ref, *state_refs):
    core = where_am_i()[2]
    for pair, lanes, t, q in tiles((qa_ref, qb_ref)):

        def causal(s, t=t):
            col = lax.broadcasted_iota(jnp.int32, s.shape, 1)
            return jnp.where(col <= row_of(t, core, s.shape), s, NEG)

        at = slice(pair * DH, (pair + 1) * DH)
        save_state(state_refs, t, lanes, step(q, kv_ref[0, :, at], kv_ref[1, :, at], causal, None))


def prev_kernel(qa_ref, qb_ref, kv_ref, o_in, l_in, m_in, out_ref):
    row, chip, core = where_am_i()
    hidden = jnp.where(row + chip > 0, 0.0, NEG)
    for pair, lanes, t, q in tiles((qa_ref, qb_ref)):
        at = slice(pair * DH, (pair + 1) * DH)
        state = load_state((o_in, l_in, m_in), t, lanes)
        out_ref[t, :, lanes] = finish(step(q, kv_ref[0, :, at], kv_ref[1, :, at], lambda s: s + hidden, state))


def mid_kernel(qa_ref, qb_ref, m0_ref, m1_ref, tab_ref, near_ref, out_ref):
    core = where_am_i()[2]
    ends = tab_ref[2:3, :CHIP]
    for pair, lanes, t, q in tiles((qa_ref, qb_ref)):
        at = slice(pair * DH, (pair + 1) * DH)

        def ended(s, t=t):
            return jnp.where(ends <= row_of(t, core, s.shape).astype(F32), s, NEG)

        k, v = (
            jnp.concatenate([ref[:, i, :, at].reshape(-1, DH) for ref in (m0_ref, m1_ref)], axis=0)
            for i in range(2)
        )
        out_ref[t, :, lanes] = near_ref[t, :, lanes] + finish(step(q, k, v, ended, None))


def far_kernel(rows, first, last, *refs):
    qa_ref, qb_ref, tab_ref = refs[:3]
    part_refs, refs = refs[3 : 3 + len(rows)], refs[3 + len(rows) :]
    state_refs, refs = ([], refs) if first else (refs[:3], refs[3:])
    for pair, lanes, t, q in tiles((qa_ref, qb_ref)):
        state = None if first else load_state(state_refs, t, lanes)
        for row, ref in zip(rows, part_refs):
            n = ref.shape[0] // 2
            for c in range(2):
                k, v = (ref[c * n : (c + 1) * n, pair, i].reshape(-1, DH) for i in range(2))
                width = k.shape[0]
                bias = tab_ref[row : row + 1, c * width : (c + 1) * width]
                state = step(q, k, v, lambda s, bias=bias: s + bias, state)
        if last:
            sum_ref, keep_ref, send_ref = refs
            (keep_ref, send_ref)[t][:, lanes] = (finish(state) + sum_ref[t, :, lanes]).astype(BF16)
        else:
            save_state(refs, t, lanes, state)


def call(kernel, name, keys, out_shape, *args):
    rows = CHIP * HEADS
    return pl.pallas_call(
        kernel,
        in_specs=[VMEM] * len(args),
        out_specs=[VMEM] * len(out_shape),
        out_shape=out_shape,
        name=name,
        compiler_params=pltpu.CompilerParams(vmem_limit_bytes=24 << 20),
        cost_estimate=pl.CostEstimate(
            flops=6 * rows * keys * DH, bytes_accessed=6 << 20, transcendentals=rows * keys
        ),
    )(*args)


def far_call(name, rows, q_own, q_got, tab, parts, *more, first=False, last=False):
    kernel = functools.partial(far_kernel, rows, first, last)
    return call(kernel, name, 1024 * len(rows), [HALF] * 2 if last else STATE, q_own, q_got, tab, *parts, *more)


def after(v, others):
    v, others = lax.optimization_barrier((v, others))
    return v, others


def body(queries, keys, values, *weights):
    kv_send, q_send, kv_own, q_own, *weights, tab = pack(queries, keys, values, *weights)
    chip_kv, mid, far = squeeze(kv_own, other_core(kv_send), *weights)
    q_send, far = after(q_send, far)
    q_got = other_core(q_send)

    far = join(far, hop(far, Z, 4))
    prev_kv = next_chip(chip_kv)
    mid = join(mid, hop(mid, X, 2))
    near = call(own_kernel, "near_own", 512, STATE, q_own, q_got, chip_kv)
    far, near = after(far, near)
    far = join(far, hop(far, Z, 1), hop(far, Z, -1), hop(far, Z, 2))
    mid = join(mid, swap_y(mid, 1))
    far = join(far, *[plane_hop(far, X, d) for d in (1, -1, 2)])
    mid_other = swap_y(mid, 2)
    (total,) = call(prev_kernel, "near_prev", 512, STATE[:1], q_own, q_got, prev_kv, *near)
    far, total = after(far, total)
    up, down = plane_hop(far, Y, 1), plane_hop(far, Y, -1)
    state = far_call("far_0", (0,), q_own, q_got, tab, [far], first=True)
    (total,) = call(mid_kernel, "mid", 512, STATE[:1], q_own, q_got, mid, mid_other, tab, total)
    far, (state, total) = after(far, (state, total))
    across = plane_hop(far, Y, 2)
    state = far_call("far_1", (1, 1), q_own, q_got, tab, [up, down], *state)
    keep, send = far_call("far_2", (0,), q_own, q_got, tab, [across], *state, total, last=True)
    return unpack(keep, other_core(send))


def solution(mesh):
    split = P(("row", "col"), None)
    return jax.shard_map(
        body,
        mesh=mesh,
        in_specs=(split, split, split, P(), P(), P(), P()),
        out_specs=split,
        check_vma=False,
    )
```

```python
import functools

import jax
import jax.numpy as jnp
import numpy as np
from jax import lax
from jax.experimental import pallas as pl
from jax.experimental.pallas import tpu as pltpu
from jax.sharding import PartitionSpec as P

HQ = 16
HK = 4
DH = 128
BLOCK = 512
MID = 8
FAR = 16
TOK = 256
CHIP = 2 * TOK
HEADS = HQ // 2
NEG = -1e30
EXP2_SCALE = float(DH**-0.5 * np.log2(np.e))
BF16 = jnp.bfloat16
F32 = jnp.float32
NT = (((1,), (1,)), ((), ()))
N_X, N_Y, N_Z = 4, 4, 8
X, Y, Z = 0, 1, 2
PACK_VMEM = 16 << 20
AXES = ("row", "col")


def place(d):
    row, col = d // 16, d % 16
    return (col // 2 % 2) * 2 + row // N_Z, col // 4, row % N_Z, col % 2


def device(x, y, z, core):
    return ((x % 2) * N_Z + z) * 16 + (y * 2 + x // 2) * 2 + core


def route(move):
    pairs = [(d, move(*place(d))) for d in range(256)]
    return [(d, device(*to)) for d, to in pairs if to is not None]


def moved(at, axis, by):
    to = list(at)
    to[axis] = (to[axis] + by) % (N_X, N_Y, N_Z)[axis]
    return to


def hop(v, axis, by):
    return lax.ppermute(v, AXES, route(lambda *at: moved(at, axis, by)))


def plane_hop(v, first, by, relayed=False):
    axes = (first, X + Y - first)

    def move(*at):
        axis = axes[at[3]]
        if axis == X and by % 2 and at[X] % 2 and not relayed:
            return None
        return moved(at, axis, by)

    return lax.ppermute(v, AXES, route(move))


def other_core(v):
    return lax.ppermute(v, AXES, [(d, d ^ 1) for d in range(256)])


def next_chip(v):
    return lax.ppermute(v, AXES, [(d, d + 2) for d in range(254)])


VMEM = pl.BlockSpec(memory_space=pltpu.VMEM)
HBM = pl.BlockSpec(memory_space=pltpu.HBM)
STATE = [jax.ShapeDtypeStruct((2, TOK, HEADS * DH), F32)] * 3
HALF = jax.ShapeDtypeStruct((TOK, HEADS * DH), BF16)
PIECE = CHIP // FAR
N_FAR = N_X * N_Z
N_MID = CHIP // MID // PIECE


def pieces(n):
    return jax.ShapeDtypeStruct((n, 2, 2, PIECE, DH), BF16)


def where_am_i():
    row, col = lax.axis_index("row"), lax.axis_index("col")
    return row, col // 2, col % 2


def own_half(core, width):
    return pl.ds(pl.multiple_of(core * width, width), width)


def copy_all(pairs, sems):
    copies = [pltpu.make_async_copy(src, dst, sems.at[i]) for i, (src, dst) in enumerate(pairs)]
    for copy in copies:
        copy.start()
    return copies


def tables(row, chip, core):
    lane = lax.broadcasted_iota(jnp.int32, (1, 1024), 1)

    def back(i):
        return jnp.where(i == 0, 0, jnp.where(i == 1, -1, jnp.where(i == 2, 1, -2)))

    y, x_hi = chip // 2, chip % 2
    x_lo, z = row // N_Z, row % N_Z
    src_z = (z + back((lane >> 6) & 3) + 4 * ((lane >> 5) & 1) + N_Z) & (N_Z - 1)
    line = jnp.where(core == 0, (x_lo + back(lane >> 8)) & 1, x_lo)
    other = jnp.where(core == 0, line, 1 - x_lo)
    coarse = [jnp.where(x * N_Z + src_z < row, 0.0, NEG) for x in (line, other)]
    late = (lane >> 6) & 3
    y_off = jnp.where(core == 0, back((lane >> 7) & 3), jnp.where(late == 0, 0, jnp.where(late == 1, -2, 2 * late - 5)))
    src_y = (y + y_off + N_Y) & (N_Y - 1)
    flip = jnp.where(core == 0, (lane >> 6) & 1, (lane >> 8) & 1)
    src = src_y * 2 + jnp.where(flip == 1, 1 - x_hi, x_hi)
    ends = (src - chip) * CHIP + (lane & 63) * MID + MID - 1
    return coarse + [ends.astype(F32)]


def pack_kernel(q_ref, k_ref, v_ref, w0, w1, w2, w3, kv_out, q_out, kv_own, q_own, x0, x1, x2, x3, tab_ref, sems):
    row, chip, core = where_am_i()
    mine, theirs = (own_half(c, 2 * DH) for c in (core, 1 - core))
    copies = copy_all(
        [(k_ref.at[:, theirs], kv_out.at[0]), (v_ref.at[:, theirs], kv_out.at[1]),
         (k_ref.at[:, mine], kv_own.at[0]), (v_ref.at[:, mine], kv_own.at[1]),
         (q_ref.at[:, own_half(1 - core, HEADS * DH)], q_out),
         (w0, x0), (w1, x1), (w2, x2), (w3, x3),
         (q_ref.at[:, own_half(core, HEADS * DH)], q_own)],
        sems,
    )
    for i, line in enumerate(tables(row, chip, core)):
        tab_ref[i : i + 1, :] = line
    for copy in copies:
        copy.wait()


def pack(q, k, v, *weights):
    kv = jax.ShapeDtypeStruct((2, TOK, 2 * DH), BF16)
    return pl.pallas_call(
        pack_kernel,
        in_specs=[HBM] * 7,
        out_specs=[VMEM] * 9,
        out_shape=[kv, HALF, kv, HALF]
        + [jax.ShapeDtypeStruct(w.shape, BF16) for w in weights]
        + [jax.ShapeDtypeStruct((8, 1024), F32)],
        scratch_shapes=[pltpu.SemaphoreType.DMA((10,))],
        name="pack",
        compiler_params=pltpu.CompilerParams(vmem_limit_bytes=PACK_VMEM),
        cost_estimate=pl.CostEstimate(flops=0, bytes_accessed=3 << 20, transcendentals=0),
    )(*(pltpu.with_memory_space_constraint(a, pltpu.HBM) for a in (q, k, v, *weights)))


def unpack_kernel(keep_ref, back_ref, out_ref, sems):
    core = where_am_i()[2]
    for copy in copy_all(
        [(keep_ref, out_ref.at[:, own_half(core, HEADS * DH)]),
         (back_ref, out_ref.at[:, own_half(1 - core, HEADS * DH)])],
        sems,
    ):
        copy.wait()


def unpack(keep, back):
    return pl.pallas_call(
        unpack_kernel,
        in_specs=[VMEM] * 2,
        out_specs=HBM,
        out_shape=jax.ShapeDtypeStruct((TOK, HQ * DH), BF16),
        scratch_shapes=[pltpu.SemaphoreType.DMA((2,))],
        name="unpack",
        compiler_params=pltpu.CompilerParams(vmem_limit_bytes=16 << 20),
        cost_estimate=pl.CostEstimate(flops=0, bytes_accessed=2 << 20, transcendentals=0),
    )(keep, back)


def join_kernel(runs, *refs):
    at = 0
    for i, start, n in runs:
        refs[-1][at : at + n] = refs[i][start : start + n]
        at += n


def join(parts, runs):
    return pl.pallas_call(
        functools.partial(join_kernel, runs),
        in_specs=[VMEM] * len(parts),
        out_specs=VMEM,
        out_shape=pieces(sum(n for _, _, n in runs)),
        name="join",
        compiler_params=pltpu.CompilerParams(vmem_limit_bytes=8 << 20),
        cost_estimate=pl.CostEstimate(flops=0, bytes_accessed=1 << 20, transcendentals=0),
    )(*parts)


def line_kernel(own_ref, prev_ref, next_ref, across_ref, line_ref, up_ref, down_ref):
    core = where_am_i()[2]
    for i, ref in enumerate((own_ref, prev_ref, next_ref, across_ref)):
        for out_ref, at in ((line_ref, 0), (up_ref, 4), (down_ref, 0)):
            out_ref[at + i * N_Z : at + (i + 1) * N_Z] = ref[:N_Z]
    mids = own_ref, across_ref, prev_ref, next_ref
    for i, ref in enumerate(mids):
        line_ref[N_FAR + 2 * i : N_FAR + 2 * i + 2] = ref[N_Z:]
    for i in range(2):
        up_ref[2 * i : 2 * i + 2] = mids[i][N_Z:]

    @pl.when(core == 0)
    def _():
        for i in range(2):
            down_ref[N_FAR + 2 * i : N_FAR + 2 * i + 2] = mids[i][N_Z:]

    @pl.when(core != 0)
    def _():
        for i in range(2):
            down_ref[N_FAR + 2 * i : N_FAR + 2 * i + 2] = mids[2 + i][N_Z:]


def lay_line(*got):
    return pl.pallas_call(
        line_kernel,
        in_specs=[VMEM] * 4,
        out_specs=[VMEM] * 3,
        out_shape=[pieces(N_FAR + 8), pieces(N_FAR + 4), pieces(N_FAR + 4)],
        name="line",
        compiler_params=pltpu.CompilerParams(vmem_limit_bytes=8 << 20),
        cost_estimate=pl.CostEstimate(flops=0, bytes_accessed=1 << 20, transcendentals=0),
    )(*got)


def squeeze_kernel(own_ref, got_ref, mk_ref, mv_ref, fk_ref, fv_ref, chip_ref, mid_ref, far_ref, x_ref):
    core = where_am_i()[2]
    for i, (m_ref, f_ref) in enumerate(((mk_ref, fk_ref), (mv_ref, fv_ref))):
        for h in range(2):
            lanes = slice(h * DH, (h + 1) * DH)
            for ref, c in ((own_ref, core), (got_ref, 1 - core)):
                at = pl.ds(pl.multiple_of(h * CHIP + c * TOK, TOK), TOK)
                x_ref[at, :] = ref[i, :, lanes].astype(F32)
            chip_ref[i, :, lanes] = x_ref[h * CHIP : (h + 1) * CHIP, :].astype(BF16)
        for run, w_ref in ((MID, m_ref), (FAR, f_ref)):
            rows = 2 * CHIP // run
            laid = jnp.concatenate(
                [x_ref[pl.ds(j, rows, stride=run), :].astype(BF16) for j in range(run)], axis=1
            )
            merged = jnp.dot(laid, w_ref[...], preferred_element_type=F32).astype(BF16)
            half = rows // 2
            for h in range(2):
                part = merged[h * half : (h + 1) * half]
                ref = mid_ref if run == MID else far_ref
                for piece in range(half // PIECE):
                    ref[piece, h, i] = part[piece * PIECE : (piece + 1) * PIECE]


def squeeze(own, got, mk, mv, fk, fv):
    return pl.pallas_call(
        squeeze_kernel,
        in_specs=[VMEM] * 6,
        out_specs=[VMEM] * 3,
        scratch_shapes=[pltpu.VMEM((2 * CHIP, DH), F32)],
        out_shape=[
            jax.ShapeDtypeStruct((2, CHIP, 2 * DH), BF16),
            pieces(CHIP // MID // PIECE),
            pieces(CHIP // FAR // PIECE),
        ],
        name="squeeze",
        compiler_params=pltpu.CompilerParams(vmem_limit_bytes=16 << 20),
        cost_estimate=pl.CostEstimate(flops=4 * 10**8, bytes_accessed=3 << 20, transcendentals=0),
    )(own, got, mk, mv, fk, fv)


def spread(x, lanes):
    return jnp.concatenate([x] * (lanes // DH), axis=1)


def step(q, k, v, fix, state):
    s = fix(lax.dot_general(q, k, NT, preferred_element_type=F32))
    top = jnp.broadcast_to(jnp.max(s, axis=1, keepdims=True), (s.shape[0], DH))
    if state is not None:
        top = jnp.maximum(top, state[0])
    p = jnp.exp2((s - spread(top, s.shape[1])) * EXP2_SCALE).astype(BF16)
    v = jnp.concatenate([v, jnp.ones(v.shape, BF16)], axis=1)
    got = jnp.dot(p, v, preferred_element_type=F32)
    if state is not None:
        got = got + state[1] * spread(jnp.exp2((state[0] - top) * EXP2_SCALE), 2 * DH)
    return top, got


def load_state(refs, t, lanes):
    o, l, m = (ref[t, :, lanes] for ref in refs)
    return m, jnp.concatenate([o, l], axis=1)


def save_state(refs, t, lanes, state):
    refs[0][t, :, lanes] = state[1][:, :DH]
    refs[1][t, :, lanes] = state[1][:, DH:]
    refs[2][t, :, lanes] = state[0]


def finish(state):
    top, got = state
    return jnp.where(top > 0.5 * NEG, got[:, :DH] / jnp.maximum(got[:, DH:], 1.0), 0.0)


def tiles(q_refs):
    for h in range(HEADS):
        lanes = slice(h * DH, (h + 1) * DH)
        for t in range(2):
            yield h // 4, lanes, t, q_refs[t][:, lanes]


def row_of(t, core, shape):
    return lax.broadcasted_iota(jnp.int32, shape, 0) + (core if t == 0 else 1 - core) * TOK


def own_kernel(qa_ref, qb_ref, kv_ref, *state_refs):
    core = where_am_i()[2]
    for pair, lanes, t, q in tiles((qa_ref, qb_ref)):

        def causal(s, t=t):
            col = lax.broadcasted_iota(jnp.int32, s.shape, 1)
            return jnp.where(col <= row_of(t, core, s.shape), s, NEG)

        at = slice(pair * DH, (pair + 1) * DH)
        save_state(state_refs, t, lanes, step(q, kv_ref[0, :, at], kv_ref[1, :, at], causal, None))


def prev_kernel(qa_ref, qb_ref, kv_ref, o_in, l_in, m_in, sum_ref, keep_ref, send_ref):
    row, chip, core = where_am_i()
    hidden = jnp.where(row + chip > 0, 0.0, NEG)
    for pair, lanes, t, q in tiles((qa_ref, qb_ref)):
        at = slice(pair * DH, (pair + 1) * DH)
        state = load_state((o_in, l_in, m_in), t, lanes)
        near = finish(step(q, kv_ref[0, :, at], kv_ref[1, :, at], lambda s: s + hidden, state))
        (keep_ref, send_ref)[t][:, lanes] = (near + sum_ref[t, :, lanes]).astype(BF16)


def mid_kernel(qa_ref, qb_ref, line_ref, up_ref, down_ref, far_up_ref, far_down_ref, tab_ref, out_ref, all_ref):
    core = where_am_i()[2]
    ends = tab_ref[2:3, :CHIP]

    def gather(*runs):
        at = 0
        for ref, start, n in runs:
            all_ref[at : at + n] = ref[start : start + n]
            at += n

    @pl.when(core == 0)
    def _():
        gather((line_ref, N_FAR, 4), (up_ref, 0, 4), (down_ref, N_FAR, 4), (far_up_ref, 0, 4))

    @pl.when(core != 0)
    def _():
        gather((line_ref, N_FAR, 8), (far_up_ref, 0, 4), (far_down_ref, N_FAR // 2, 4))

    for pair, lanes, t, q in tiles((qa_ref, qb_ref)):

        def ended(s, t=t):
            return jnp.where(ends <= row_of(t, core, s.shape).astype(F32), s, NEG)

        k, v = (all_ref[:, pair, i].reshape(-1, DH) for i in range(2))
        out_ref[t, :, lanes] = finish(step(q, k, v, ended, None))


def far_kernel(steps, n_refs, first, last, *refs):
    qa_ref, qb_ref, tab_ref = refs[:3]
    part_refs, refs = refs[3 : 3 + n_refs], refs[3 + n_refs :]
    state_refs, refs = ([], refs) if first else (refs[:3], refs[3:])
    for pair, lanes, t, q in tiles((qa_ref, qb_ref)):
        state = None if first else load_state(state_refs, t, lanes)
        for i, start, n, row, lane in steps:
            k, v = (part_refs[i][start : start + n, pair, j].reshape(-1, DH) for j in range(2))
            bias = tab_ref[row : row + 1, lane : lane + n * PIECE]
            state = step(q, k, v, lambda s, bias=bias: s + bias, state)
        if last:
            sum_ref, out_ref = refs
            out_ref[t, :, lanes] = finish(state) + sum_ref[t, :, lanes]
        else:
            save_state(refs, t, lanes, state)


def call(kernel, name, keys, out_shape, *args, scratch=()):
    rows = CHIP * HEADS
    return pl.pallas_call(
        kernel,
        in_specs=[VMEM] * len(args),
        out_specs=[VMEM] * len(out_shape),
        out_shape=out_shape,
        scratch_shapes=scratch,
        name=name,
        compiler_params=pltpu.CompilerParams(vmem_limit_bytes=24 << 20),
        cost_estimate=pl.CostEstimate(
            flops=6 * rows * keys * DH, bytes_accessed=6 << 20, transcendentals=rows * keys
        ),
    )(*args)


def far_call(name, steps, q_own, q_got, tab, parts, *more, first=False, last=False):
    kernel = functools.partial(far_kernel, steps, len(parts), first, last)
    keys = PIECE * sum(n for _, _, n, _, _ in steps)
    return call(kernel, name, keys, STATE[:1] if last else STATE, q_own, q_got, tab, *parts, *more)


def after(v, others):
    v, others = lax.optimization_barrier((v, others))
    return v, others


def body(queries, keys, values, *weights):
    kv_send, q_send, kv_own, q_own, *weights, tab = pack(queries, keys, values, *weights)
    chip_kv, mid, far = squeeze(kv_own, other_core(kv_send), *weights)
    q_send, far = after(q_send, far)
    q_got = other_core(q_send)

    near = call(own_kernel, "near_own", 512, STATE, q_own, q_got, chip_kv)
    got, near = after(hop(far, Z, 4), near)
    far = join([far, got], [(0, 0, 1), (1, 0, 1)])
    got = [hop(far, Z, d) for d in (1, -1, 2)]
    far = join([far, *got, mid], [(0, 0, 2), (1, 0, 2), (2, 0, 2), (3, 0, 2), (4, 0, N_MID)])
    got = [plane_hop(far, X, d) for d in (1, -1, 2)]
    line, up, down = lay_line(far, *got)
    up, down = plane_hop(up, Y, 1, True), plane_hop(down, Y, -1, True)
    state = far_call("far_0", [(0, 0, 16, 0, 0), (0, 16, 16, 0, 512)], q_own, q_got, tab, [line], first=True)
    (up, down), state = after((up, down), state)
    far_up = plane_hop(join([up], [(0, 0, 20)]), Y, 1, True)
    far_down = plane_hop(join([down], [(0, 16, 20)]), Y, -1, True)
    state = far_call(
        "far_1",
        [(0, 4, 16, 1, 0), (0, 20, 16, 1, 512), (1, 0, 16, 1, 0), (1, 16, 16, 1, 512)],
        q_own, q_got, tab, [up, down], *state,
    )
    chip_kv, state = after(chip_kv, state)
    prev_kv = next_chip(chip_kv)
    (total,) = call(
        mid_kernel, "mid", 512, STATE[:1], q_own, q_got, line, up, down, far_up, far_down, tab,
        scratch=[pltpu.VMEM(pieces(8 * N_MID).shape, BF16)],
    )
    (total,) = far_call(
        "far_2", [(0, 4, 16, 0, 0), (1, 0, 16, 0, 512)], q_own, q_got, tab, [far_up, far_down], *state, total, last=True
    )
    keep, send = call(prev_kernel, "near_prev", 512, [HALF] * 2, q_own, q_got, prev_kv, *near, total)
    return unpack(keep, other_core(send))


def solution(mesh):
    split = P(("row", "col"), None)
    return jax.shard_map(
        body,
        mesh=mesh,
        in_specs=(split, split, split, P(), P(), P(), P()),
        out_specs=split,
        check_vma=False,
    )
```

```python
import functools

import jax
import jax.numpy as jnp
import numpy as np
from jax import lax
from jax.experimental import pallas as pl
from jax.experimental.pallas import tpu as pltpu
from jax.sharding import PartitionSpec as P

HQ = 16
HK = 4
DH = 128
BLOCK = 512
MID = 8
FAR = 16
TOK = 256
CHIP = 2 * TOK
HEADS = HQ // 2
NEG = -1e30
EXP2_SCALE = float(DH**-0.5 * np.log2(np.e))
BF16 = jnp.bfloat16
F32 = jnp.float32
NT = (((1,), (1,)), ((), ()))
N_X, N_Y, N_Z = 4, 4, 8
X, Y, Z = 0, 1, 2
PACK_VMEM = 16 << 20
AXES = ("row", "col")


def place(d):
    row, col = d // 16, d % 16
    return (col // 2 % 2) * 2 + row // N_Z, col // 4, row % N_Z, col % 2


def device(x, y, z, core):
    return ((x % 2) * N_Z + z) * 16 + (y * 2 + x // 2) * 2 + core


def route(move):
    pairs = [(d, move(*place(d))) for d in range(256)]
    return [(d, device(*to)) for d, to in pairs if to is not None]


def moved(at, axis, by):
    to = list(at)
    to[axis] = (to[axis] + by) % (N_X, N_Y, N_Z)[axis]
    return to


def hop(v, axis, by):
    return lax.ppermute(v, AXES, route(lambda *at: moved(at, axis, by)))


def plane_hop(v, first, by, relayed=False):
    axes = (first, X + Y - first)

    def move(*at):
        axis = axes[at[3]]
        if axis == X and by % 2 and at[X] % 2 and not relayed:
            return None
        return moved(at, axis, by)

    return lax.ppermute(v, AXES, route(move))


def other_core(v):
    return lax.ppermute(v, AXES, [(d, d ^ 1) for d in range(256)])


def next_chip(v):
    return lax.ppermute(v, AXES, [(d, d + 2) for d in range(254)])


VMEM = pl.BlockSpec(memory_space=pltpu.VMEM)
HBM = pl.BlockSpec(memory_space=pltpu.HBM)
STATE = [jax.ShapeDtypeStruct((2, TOK, HEADS * DH), F32)] * 3
HALF = jax.ShapeDtypeStruct((TOK, HEADS * DH), BF16)
PIECE = CHIP // FAR
N_FAR = N_X * N_Z
N_MID = CHIP // MID // PIECE


def pieces(n):
    return jax.ShapeDtypeStruct((n, 2, 2, PIECE, DH), BF16)


def where_am_i():
    row, col = lax.axis_index("row"), lax.axis_index("col")
    return row, col // 2, col % 2


def own_half(core, width):
    return pl.ds(pl.multiple_of(core * width, width), width)


def copy_all(pairs, sems):
    copies = [pltpu.make_async_copy(src, dst, sems.at[i]) for i, (src, dst) in enumerate(pairs)]
    for copy in copies:
        copy.start()
    return copies


def tables(row, chip, core):
    lane = lax.broadcasted_iota(jnp.int32, (1, 1024), 1)

    def back(i):
        return jnp.where(i == 0, 0, jnp.where(i == 1, -1, jnp.where(i == 2, 1, -2)))

    y, x_hi = chip // 2, chip % 2
    x_lo, z = row // N_Z, row % N_Z
    src_z = (z + back((lane >> 6) & 3) + 4 * ((lane >> 5) & 1) + N_Z) & (N_Z - 1)
    line = jnp.where(core == 0, (x_lo + back(lane >> 8)) & 1, x_lo)
    other = jnp.where(core == 0, line, 1 - x_lo)
    coarse = [jnp.where(x * N_Z + src_z < row, 0.0, NEG) for x in (line, other)]
    late = (lane >> 6) & 3
    y_off = jnp.where(core == 0, back((lane >> 7) & 3), jnp.where(late == 0, 0, jnp.where(late == 1, -2, 2 * late - 5)))
    src_y = (y + y_off + N_Y) & (N_Y - 1)
    flip = jnp.where(core == 0, (lane >> 6) & 1, (lane >> 8) & 1)
    src = src_y * 2 + jnp.where(flip == 1, 1 - x_hi, x_hi)
    ends = (src - chip) * CHIP + (lane & 63) * MID + MID - 1
    return coarse + [ends.astype(F32)]


def pack_kernel(q_ref, k_ref, v_ref, w0, w1, w2, w3, kv_out, q_out, kv_own, q_own, x0, x1, x2, x3, tab_ref, sems):
    row, chip, core = where_am_i()
    mine, theirs = (own_half(c, 2 * DH) for c in (core, 1 - core))
    copies = copy_all(
        [(k_ref.at[:, theirs], kv_out.at[0]), (v_ref.at[:, theirs], kv_out.at[1]),
         (k_ref.at[:, mine], kv_own.at[0]), (v_ref.at[:, mine], kv_own.at[1]),
         (q_ref.at[:, own_half(1 - core, HEADS * DH)], q_out),
         (w0, x0), (w1, x1), (w2, x2), (w3, x3),
         (q_ref.at[:, own_half(core, HEADS * DH)], q_own)],
        sems,
    )
    for i, line in enumerate(tables(row, chip, core)):
        tab_ref[i : i + 1, :] = line
    for copy in copies:
        copy.wait()


def pack(q, k, v, *weights):
    kv = jax.ShapeDtypeStruct((2, TOK, 2 * DH), BF16)
    return pl.pallas_call(
        pack_kernel,
        in_specs=[HBM] * 7,
        out_specs=[VMEM] * 9,
        out_shape=[kv, HALF, kv, HALF]
        + [jax.ShapeDtypeStruct(w.shape, BF16) for w in weights]
        + [jax.ShapeDtypeStruct((8, 1024), F32)],
        scratch_shapes=[pltpu.SemaphoreType.DMA((10,))],
        name="pack",
        compiler_params=pltpu.CompilerParams(vmem_limit_bytes=PACK_VMEM),
        cost_estimate=pl.CostEstimate(flops=0, bytes_accessed=3 << 20, transcendentals=0),
    )(*(pltpu.with_memory_space_constraint(a, pltpu.HBM) for a in (q, k, v, *weights)))


def unpack_kernel(keep_ref, back_ref, out_ref, sems):
    core = where_am_i()[2]
    for copy in copy_all(
        [(keep_ref, out_ref.at[:, own_half(core, HEADS * DH)]),
         (back_ref, out_ref.at[:, own_half(1 - core, HEADS * DH)])],
        sems,
    ):
        copy.wait()


def unpack(keep, back):
    return pl.pallas_call(
        unpack_kernel,
        in_specs=[VMEM] * 2,
        out_specs=HBM,
        out_shape=jax.ShapeDtypeStruct((TOK, HQ * DH), BF16),
        scratch_shapes=[pltpu.SemaphoreType.DMA((2,))],
        name="unpack",
        compiler_params=pltpu.CompilerParams(vmem_limit_bytes=16 << 20),
        cost_estimate=pl.CostEstimate(flops=0, bytes_accessed=2 << 20, transcendentals=0),
    )(keep, back)


def join_kernel(runs, *refs):
    at = 0
    for i, start, n in runs:
        refs[-1][at : at + n] = refs[i][start : start + n]
        at += n


def join(parts, runs):
    return pl.pallas_call(
        functools.partial(join_kernel, runs),
        in_specs=[VMEM] * len(parts),
        out_specs=VMEM,
        out_shape=pieces(sum(n for _, _, n in runs)),
        name="join",
        compiler_params=pltpu.CompilerParams(vmem_limit_bytes=8 << 20),
        cost_estimate=pl.CostEstimate(flops=0, bytes_accessed=1 << 20, transcendentals=0),
    )(*parts)


def line_kernel(own_ref, prev_ref, next_ref, across_ref, line_ref, up_a, down_a, up_b, down_b):
    core = where_am_i()[2]
    half = N_FAR // 2
    for i, ref in enumerate((own_ref, prev_ref, next_ref, across_ref)):
        line_ref[i * N_Z : (i + 1) * N_Z] = ref[:N_Z]
        for out_ref, at in ((up_a, 4), (down_b, 0)) if i < 2 else ((down_a, 0), (up_b, 0)):
            out_ref[at + i % 2 * N_Z : at + (i % 2 + 1) * N_Z] = ref[:N_Z]
    mids = own_ref, across_ref, prev_ref, next_ref
    for i, ref in enumerate(mids):
        line_ref[N_FAR + 2 * i : N_FAR + 2 * i + 2] = ref[N_Z:]
    for i in range(2):
        up_a[2 * i : 2 * i + 2] = mids[i][N_Z:]

    @pl.when(core == 0)
    def _():
        for i in range(2):
            down_a[half + 2 * i : half + 2 * i + 2] = mids[i][N_Z:]

    @pl.when(core != 0)
    def _():
        for i in range(2):
            down_a[half + 2 * i : half + 2 * i + 2] = mids[2 + i][N_Z:]


def lay_line(*got):
    half = N_FAR // 2
    return pl.pallas_call(
        line_kernel,
        in_specs=[VMEM] * 4,
        out_specs=[VMEM] * 5,
        out_shape=[pieces(N_FAR + 8), pieces(half + 4), pieces(half + 4), pieces(half), pieces(half)],
        name="line",
        compiler_params=pltpu.CompilerParams(vmem_limit_bytes=8 << 20),
        cost_estimate=pl.CostEstimate(flops=0, bytes_accessed=1 << 20, transcendentals=0),
    )(*got)


def squeeze_kernel(own_ref, got_ref, mk_ref, mv_ref, fk_ref, fv_ref, chip_ref, mid_ref, far_ref, x_ref):
    core = where_am_i()[2]
    for i, (m_ref, f_ref) in enumerate(((mk_ref, fk_ref), (mv_ref, fv_ref))):
        for h in range(2):
            lanes = slice(h * DH, (h + 1) * DH)
            for ref, c in ((own_ref, core), (got_ref, 1 - core)):
                at = pl.ds(pl.multiple_of(h * CHIP + c * TOK, TOK), TOK)
                x_ref[at, :] = ref[i, :, lanes].astype(F32)
            chip_ref[i, :, lanes] = x_ref[h * CHIP : (h + 1) * CHIP, :].astype(BF16)
        for run, w_ref in ((MID, m_ref), (FAR, f_ref)):
            rows = 2 * CHIP // run
            laid = jnp.concatenate(
                [x_ref[pl.ds(j, rows, stride=run), :].astype(BF16) for j in range(run)], axis=1
            )
            merged = jnp.dot(laid, w_ref[...], preferred_element_type=F32).astype(BF16)
            half = rows // 2
            for h in range(2):
                part = merged[h * half : (h + 1) * half]
                ref = mid_ref if run == MID else far_ref
                for piece in range(half // PIECE):
                    ref[piece, h, i] = part[piece * PIECE : (piece + 1) * PIECE]


def squeeze(own, got, mk, mv, fk, fv):
    return pl.pallas_call(
        squeeze_kernel,
        in_specs=[VMEM] * 6,
        out_specs=[VMEM] * 3,
        scratch_shapes=[pltpu.VMEM((2 * CHIP, DH), F32)],
        out_shape=[
            jax.ShapeDtypeStruct((2, CHIP, 2 * DH), BF16),
            pieces(CHIP // MID // PIECE),
            pieces(CHIP // FAR // PIECE),
        ],
        name="squeeze",
        compiler_params=pltpu.CompilerParams(vmem_limit_bytes=16 << 20),
        cost_estimate=pl.CostEstimate(flops=4 * 10**8, bytes_accessed=3 << 20, transcendentals=0),
    )(own, got, mk, mv, fk, fv)


def spread(x, lanes):
    return jnp.concatenate([x] * (lanes // DH), axis=1)


def step(q, k, v, fix, state):
    s = fix(lax.dot_general(q, k, NT, preferred_element_type=F32))
    top = jnp.broadcast_to(jnp.max(s, axis=1, keepdims=True), (s.shape[0], DH))
    if state is not None:
        top = jnp.maximum(top, state[0])
    p = jnp.exp2((s - spread(top, s.shape[1])) * EXP2_SCALE).astype(BF16)
    v = jnp.concatenate([v, jnp.ones(v.shape, BF16)], axis=1)
    got = jnp.dot(p, v, preferred_element_type=F32)
    if state is not None:
        got = got + state[1] * spread(jnp.exp2((state[0] - top) * EXP2_SCALE), 2 * DH)
    return top, got


def load_state(refs, t, lanes):
    o, l, m = (ref[t, :, lanes] for ref in refs)
    return m, jnp.concatenate([o, l], axis=1)


def save_state(refs, t, lanes, state):
    refs[0][t, :, lanes] = state[1][:, :DH]
    refs[1][t, :, lanes] = state[1][:, DH:]
    refs[2][t, :, lanes] = state[0]


def finish(state):
    top, got = state
    return jnp.where(top > 0.5 * NEG, got[:, :DH] / jnp.maximum(got[:, DH:], 1.0), 0.0)


def tiles(q_refs):
    for h in range(HEADS):
        lanes = slice(h * DH, (h + 1) * DH)
        for t in range(2):
            yield h // 4, lanes, t, q_refs[t][:, lanes]


def row_of(t, core, shape):
    return lax.broadcasted_iota(jnp.int32, shape, 0) + (core if t == 0 else 1 - core) * TOK


def own_kernel(qa_ref, qb_ref, kv_ref, *state_refs):
    core = where_am_i()[2]
    for pair, lanes, t, q in tiles((qa_ref, qb_ref)):

        def causal(s, t=t):
            col = lax.broadcasted_iota(jnp.int32, s.shape, 1)
            return jnp.where(col <= row_of(t, core, s.shape), s, NEG)

        at = slice(pair * DH, (pair + 1) * DH)
        save_state(state_refs, t, lanes, step(q, kv_ref[0, :, at], kv_ref[1, :, at], causal, None))


def prev_kernel(qa_ref, qb_ref, kv_ref, o_in, l_in, m_in, sum_ref, keep_ref, send_ref):
    row, chip, core = where_am_i()
    hidden = jnp.where(row + chip > 0, 0.0, NEG)
    for pair, lanes, t, q in tiles((qa_ref, qb_ref)):
        at = slice(pair * DH, (pair + 1) * DH)
        state = load_state((o_in, l_in, m_in), t, lanes)
        near = finish(step(q, kv_ref[0, :, at], kv_ref[1, :, at], lambda s: s + hidden, state))
        (keep_ref, send_ref)[t][:, lanes] = (near + sum_ref[t, :, lanes]).astype(BF16)


def mid_kernel(qa_ref, qb_ref, line_ref, up_ref, down_ref, far_up_ref, far_down_ref, tab_ref, out_ref, all_ref):
    core = where_am_i()[2]
    ends = tab_ref[2:3, :CHIP]

    def gather(*runs):
        at = 0
        for ref, start, n in runs:
            all_ref[at : at + n] = ref[start : start + n]
            at += n

    @pl.when(core == 0)
    def _():
        gather((line_ref, N_FAR, 4), (up_ref, 0, 4), (down_ref, N_FAR // 2, 4), (far_up_ref, 0, 4))

    @pl.when(core != 0)
    def _():
        gather((line_ref, N_FAR, 8), (far_up_ref, 0, 4), (far_down_ref, N_FAR // 2, 4))

    for pair, lanes, t, q in tiles((qa_ref, qb_ref)):

        def ended(s, t=t):
            return jnp.where(ends <= row_of(t, core, s.shape).astype(F32), s, NEG)

        k, v = (all_ref[:, pair, i].reshape(-1, DH) for i in range(2))
        out_ref[t, :, lanes] = finish(step(q, k, v, ended, None))


def far_kernel(steps, n_refs, first, last, *refs):
    qa_ref, qb_ref, tab_ref = refs[:3]
    part_refs, refs = refs[3 : 3 + n_refs], refs[3 + n_refs :]
    state_refs, refs = ([], refs) if first else (refs[:3], refs[3:])
    for pair, lanes, t, q in tiles((qa_ref, qb_ref)):
        state = None if first else load_state(state_refs, t, lanes)
        for i, start, n, row, lane in steps:
            k, v = (part_refs[i][start : start + n, pair, j].reshape(-1, DH) for j in range(2))
            bias = tab_ref[row : row + 1, lane : lane + n * PIECE]
            state = step(q, k, v, lambda s, bias=bias: s + bias, state)
        if last:
            sum_ref, out_ref = refs
            out_ref[t, :, lanes] = finish(state) + sum_ref[t, :, lanes]
        else:
            save_state(refs, t, lanes, state)


def call(kernel, name, keys, out_shape, *args, scratch=()):
    rows = CHIP * HEADS
    return pl.pallas_call(
        kernel,
        in_specs=[VMEM] * len(args),
        out_specs=[VMEM] * len(out_shape),
        out_shape=out_shape,
        scratch_shapes=scratch,
        name=name,
        compiler_params=pltpu.CompilerParams(vmem_limit_bytes=24 << 20),
        cost_estimate=pl.CostEstimate(
            flops=6 * rows * keys * DH, bytes_accessed=6 << 20, transcendentals=rows * keys
        ),
    )(*args)


def far_call(name, steps, q_own, q_got, tab, parts, *more, first=False, last=False):
    kernel = functools.partial(far_kernel, steps, len(parts), first, last)
    keys = PIECE * sum(n for _, _, n, _, _ in steps)
    return call(kernel, name, keys, STATE[:1] if last else STATE, q_own, q_got, tab, *parts, *more)


def after(v, others):
    v, others = lax.optimization_barrier((v, others))
    return v, others


def body(queries, keys, values, *weights):
    kv_send, q_send, kv_own, q_own, *weights, tab = pack(queries, keys, values, *weights)
    chip_kv, mid, far = squeeze(kv_own, other_core(kv_send), *weights)
    q_send, far = after(q_send, far)
    q_got = other_core(q_send)

    near = call(own_kernel, "near_own", 512, STATE, q_own, q_got, chip_kv)
    got, near = after(hop(far, Z, 4), near)
    far = join([far, got], [(0, 0, 1), (1, 0, 1)])
    got = [hop(far, Z, d) for d in (1, -1, 2)]
    far = join([far, *got, mid], [(0, 0, 2), (1, 0, 2), (2, 0, 2), (3, 0, 2), (4, 0, N_MID)])
    got = [plane_hop(far, X, d) for d in (1, -1, 2)]
    line, up_a, down_a, up_b, down_b = lay_line(far, *[plane_hop(far, X, d) for d in (1, -1, 2)])
    up_a, down_a = plane_hop(up_a, Y, 1, True), plane_hop(down_a, Y, -1, True)
    up_b, down_b = plane_hop(up_b, Y, 1, True), plane_hop(down_b, Y, -1, True)
    state = far_call("far_0", [(0, 0, 16, 0, 0), (0, 16, 16, 0, 512)], q_own, q_got, tab, [line], first=True)
    (up_a, down_a), state = after((up_a, down_a), state)
    far_up, far_down = plane_hop(up_a, Y, 1, True), plane_hop(down_a, Y, -1, True)
    state = far_call("far_a", [(0, 4, 16, 1, 0), (1, 0, 16, 1, 512)], q_own, q_got, tab, [up_a, down_a], *state)
    (up_b, down_b), state = after((up_b, down_b), state)
    chip_kv, state = after(chip_kv, state)
    prev_kv = next_chip(chip_kv)
    state = far_call("far_b", [(0, 0, 16, 1, 512), (1, 0, 16, 1, 0)], q_own, q_got, tab, [up_b, down_b], *state)
    (total,) = call(
        mid_kernel, "mid", 512, STATE[:1], q_own, q_got, line, up_a, down_a, far_up, far_down, tab,
        scratch=[pltpu.VMEM(pieces(8 * N_MID).shape, BF16)],
    )
    (total,) = far_call(
        "far_2", [(0, 4, 16, 0, 0), (1, 0, 16, 0, 512)], q_own, q_got, tab, [far_up, far_down], *state, total, last=True
    )
    keep, send = call(prev_kernel, "near_prev", 512, [HALF] * 2, q_own, q_got, prev_kv, *near, total)
    return unpack(keep, other_core(send))


def solution(mesh):
    split = P(("row", "col"), None)
    return jax.shard_map(
        body,
        mesh=mesh,
        in_specs=(split, split, split, P(), P(), P(), P()),
        out_specs=split,
        check_vma=False,
    )
```

```python
import functools

import jax
import jax.numpy as jnp
import numpy as np
from jax import lax
from jax.experimental import pallas as pl
from jax.experimental.pallas import tpu as pltpu
from jax.sharding import PartitionSpec as P

HQ = 16
HK = 4
DH = 128
BLOCK = 512
MID = 8
FAR = 16
TOK = 256
CHIP = 2 * TOK
HEADS = HQ // 2
NEG = -1e30
EXP2_SCALE = float(DH**-0.5 * np.log2(np.e))
BF16 = jnp.bfloat16
F32 = jnp.float32
NT = (((1,), (1,)), ((), ()))
N_X, N_Y, N_Z = 4, 4, 8
X, Y, Z = 0, 1, 2
PACK_VMEM = 16 << 20
AXES = ("row", "col")


def place(d):
    row, col = d // 16, d % 16
    return (col // 2 % 2) * 2 + row // N_Z, col // 4, row % N_Z, col % 2


def device(x, y, z, core):
    return ((x % 2) * N_Z + z) * 16 + (y * 2 + x // 2) * 2 + core


def route(move):
    pairs = [(d, move(*place(d))) for d in range(256)]
    return [(d, device(*to)) for d, to in pairs if to is not None]


def moved(at, axis, by):
    to = list(at)
    to[axis] = (to[axis] + by) % (N_X, N_Y, N_Z)[axis]
    return to


def hop(v, axis, by):
    return lax.ppermute(v, AXES, route(lambda *at: moved(at, axis, by)))


def plane_hop(v, first, by, relayed=False):
    axes = (first, X + Y - first)

    def move(*at):
        axis = axes[at[3]]
        if axis == X and by % 2 and at[X] % 2 and not relayed:
            return None
        return moved(at, axis, by)

    return lax.ppermute(v, AXES, route(move))


def other_core(v):
    return lax.ppermute(v, AXES, [(d, d ^ 1) for d in range(256)])


def next_chip(v):
    return lax.ppermute(v, AXES, [(d, d + 2) for d in range(254)])


VMEM = pl.BlockSpec(memory_space=pltpu.VMEM)
HBM = pl.BlockSpec(memory_space=pltpu.HBM)
STATE = [jax.ShapeDtypeStruct((2, TOK, HEADS * DH), F32)] * 3
HALF = jax.ShapeDtypeStruct((TOK, HEADS * DH), BF16)
PIECE = CHIP // FAR
N_FAR = N_X * N_Z
N_MID = CHIP // MID // PIECE


def pieces(n):
    return jax.ShapeDtypeStruct((n, 2, 2, PIECE, DH), BF16)


def where_am_i():
    row, col = lax.axis_index("row"), lax.axis_index("col")
    return row, col // 2, col % 2


def own_half(core, width):
    return pl.ds(pl.multiple_of(core * width, width), width)


def copy_all(pairs, sems):
    copies = [pltpu.make_async_copy(src, dst, sems.at[i]) for i, (src, dst) in enumerate(pairs)]
    for copy in copies:
        copy.start()
    return copies


def tables(row, chip, core):
    lane = lax.broadcasted_iota(jnp.int32, (1, 1024), 1)

    def back(i):
        return jnp.where(i == 0, 0, jnp.where(i == 1, -1, jnp.where(i == 2, 1, -2)))

    y, x_hi = chip // 2, chip % 2
    x_lo, z = row // N_Z, row % N_Z
    src_z = (z + back((lane >> 6) & 3) + 4 * ((lane >> 5) & 1) + N_Z) & (N_Z - 1)
    line = jnp.where(core == 0, (x_lo + (lane >> 9)) & 1, x_lo)
    other = jnp.where(core == 0, line, 1 - x_lo)
    coarse = [jnp.where(x * N_Z + src_z < row, 0.0, NEG) for x in (line, other)]
    late = (lane >> 6) & 3
    y_off = jnp.where(core == 0, back((lane >> 7) & 3), jnp.where(late == 0, 0, jnp.where(late == 1, -2, 2 * late - 5)))
    src_y = (y + y_off + N_Y) & (N_Y - 1)
    flip = jnp.where(core == 0, (lane >> 6) & 1, (lane >> 8) & 1)
    src = src_y * 2 + jnp.where(flip == 1, 1 - x_hi, x_hi)
    ends = (src - chip) * CHIP + (lane & 63) * MID + MID - 1
    return coarse + [ends.astype(F32)]


def pack_kernel(q_ref, k_ref, v_ref, w0, w1, w2, w3, kv_out, q_out, kv_own, q_own, x0, x1, x2, x3, tab_ref, sems):
    row, chip, core = where_am_i()
    mine, theirs = (own_half(c, 2 * DH) for c in (core, 1 - core))
    copies = copy_all(
        [(k_ref.at[:, theirs], kv_out.at[0]), (v_ref.at[:, theirs], kv_out.at[1]),
         (k_ref.at[:, mine], kv_own.at[0]), (v_ref.at[:, mine], kv_own.at[1]),
         (q_ref.at[:, own_half(1 - core, HEADS * DH)], q_out),
         (w0, x0), (w1, x1), (w2, x2), (w3, x3),
         (q_ref.at[:, own_half(core, HEADS * DH)], q_own)],
        sems,
    )
    for i, line in enumerate(tables(row, chip, core)):
        tab_ref[i : i + 1, :] = line
    for copy in copies:
        copy.wait()


def pack(q, k, v, *weights):
    kv = jax.ShapeDtypeStruct((2, TOK, 2 * DH), BF16)
    return pl.pallas_call(
        pack_kernel,
        in_specs=[HBM] * 7,
        out_specs=[VMEM] * 9,
        out_shape=[kv, HALF, kv, HALF]
        + [jax.ShapeDtypeStruct(w.shape, BF16) for w in weights]
        + [jax.ShapeDtypeStruct((8, 1024), F32)],
        scratch_shapes=[pltpu.SemaphoreType.DMA((10,))],
        name="pack",
        compiler_params=pltpu.CompilerParams(vmem_limit_bytes=PACK_VMEM),
        cost_estimate=pl.CostEstimate(flops=0, bytes_accessed=3 << 20, transcendentals=0),
    )(*(pltpu.with_memory_space_constraint(a, pltpu.HBM) for a in (q, k, v, *weights)))


def unpack_kernel(keep_ref, back_ref, out_ref, sems):
    core = where_am_i()[2]
    for copy in copy_all(
        [(keep_ref, out_ref.at[:, own_half(core, HEADS * DH)]),
         (back_ref, out_ref.at[:, own_half(1 - core, HEADS * DH)])],
        sems,
    ):
        copy.wait()


def unpack(keep, back):
    return pl.pallas_call(
        unpack_kernel,
        in_specs=[VMEM] * 2,
        out_specs=HBM,
        out_shape=jax.ShapeDtypeStruct((TOK, HQ * DH), BF16),
        scratch_shapes=[pltpu.SemaphoreType.DMA((2,))],
        name="unpack",
        compiler_params=pltpu.CompilerParams(vmem_limit_bytes=16 << 20),
        cost_estimate=pl.CostEstimate(flops=0, bytes_accessed=2 << 20, transcendentals=0),
    )(keep, back)


def join_kernel(runs, *refs):
    at = 0
    for i, start, n in runs:
        refs[-1][at : at + n] = refs[i][start : start + n]
        at += n


def join(parts, runs):
    return pl.pallas_call(
        functools.partial(join_kernel, runs),
        in_specs=[VMEM] * len(parts),
        out_specs=VMEM,
        out_shape=pieces(sum(n for _, _, n in runs)),
        name="join",
        compiler_params=pltpu.CompilerParams(vmem_limit_bytes=8 << 20),
        cost_estimate=pl.CostEstimate(flops=0, bytes_accessed=1 << 20, transcendentals=0),
    )(*parts)


def line_kernel(own_ref, prev_ref, next_ref, across_ref, line_ref, up_a, down_a, up_b, down_b):
    core = where_am_i()[2]
    half = N_FAR // 2
    for i, ref in enumerate((own_ref, across_ref, prev_ref, next_ref)):
        line_ref[i * N_Z : (i + 1) * N_Z] = ref[:N_Z]
        for out_ref, at in ((up_a, 4), (down_b, 0)) if i < 2 else ((down_a, 0), (up_b, 0)):
            out_ref[at + i % 2 * N_Z : at + (i % 2 + 1) * N_Z] = ref[:N_Z]
    mids = own_ref, across_ref, prev_ref, next_ref
    for i, ref in enumerate(mids):
        line_ref[N_FAR + 2 * i : N_FAR + 2 * i + 2] = ref[N_Z:]
    for i in range(2):
        up_a[2 * i : 2 * i + 2] = mids[i][N_Z:]

    @pl.when(core == 0)
    def _():
        for i in range(2):
            down_a[half + 2 * i : half + 2 * i + 2] = mids[i][N_Z:]

    @pl.when(core != 0)
    def _():
        for i in range(2):
            down_a[half + 2 * i : half + 2 * i + 2] = mids[2 + i][N_Z:]


def lay_line(*got):
    half = N_FAR // 2
    return pl.pallas_call(
        line_kernel,
        in_specs=[VMEM] * 4,
        out_specs=[VMEM] * 5,
        out_shape=[pieces(N_FAR + 8), pieces(half + 4), pieces(half + 4), pieces(half), pieces(half)],
        name="line",
        compiler_params=pltpu.CompilerParams(vmem_limit_bytes=8 << 20),
        cost_estimate=pl.CostEstimate(flops=0, bytes_accessed=1 << 20, transcendentals=0),
    )(*got)


def squeeze_kernel(own_ref, got_ref, mk_ref, mv_ref, fk_ref, fv_ref, chip_ref, mid_ref, far_ref, x_ref):
    core = where_am_i()[2]
    for i, (m_ref, f_ref) in enumerate(((mk_ref, fk_ref), (mv_ref, fv_ref))):
        for h in range(2):
            lanes = slice(h * DH, (h + 1) * DH)
            for ref, c in ((own_ref, core), (got_ref, 1 - core)):
                at = pl.ds(pl.multiple_of(h * CHIP + c * TOK, TOK), TOK)
                x_ref[at, :] = ref[i, :, lanes].astype(F32)
            chip_ref[i, :, lanes] = x_ref[h * CHIP : (h + 1) * CHIP, :].astype(BF16)
        for run, w_ref in ((MID, m_ref), (FAR, f_ref)):
            rows = 2 * CHIP // run
            laid = jnp.concatenate(
                [x_ref[pl.ds(j, rows, stride=run), :].astype(BF16) for j in range(run)], axis=1
            )
            merged = jnp.dot(laid, w_ref[...], preferred_element_type=F32).astype(BF16)
            half = rows // 2
            for h in range(2):
                part = merged[h * half : (h + 1) * half]
                ref = mid_ref if run == MID else far_ref
                for piece in range(half // PIECE):
                    ref[piece, h, i] = part[piece * PIECE : (piece + 1) * PIECE]


def squeeze(own, got, mk, mv, fk, fv):
    return pl.pallas_call(
        squeeze_kernel,
        in_specs=[VMEM] * 6,
        out_specs=[VMEM] * 3,
        scratch_shapes=[pltpu.VMEM((2 * CHIP, DH), F32)],
        out_shape=[
            jax.ShapeDtypeStruct((2, CHIP, 2 * DH), BF16),
            pieces(CHIP // MID // PIECE),
            pieces(CHIP // FAR // PIECE),
        ],
        name="squeeze",
        compiler_params=pltpu.CompilerParams(vmem_limit_bytes=16 << 20),
        cost_estimate=pl.CostEstimate(flops=4 * 10**8, bytes_accessed=3 << 20, transcendentals=0),
    )(own, got, mk, mv, fk, fv)


def spread(x, lanes):
    return jnp.concatenate([x] * (lanes // DH), axis=1)


def step(q, k, v, fix, state):
    s = fix(lax.dot_general(q, k, NT, preferred_element_type=F32))
    top = jnp.broadcast_to(jnp.max(s, axis=1, keepdims=True), (s.shape[0], DH))
    if state is not None:
        top = jnp.maximum(top, state[0])
    p = jnp.exp2((s - spread(top, s.shape[1])) * EXP2_SCALE).astype(BF16)
    v = jnp.concatenate([v, jnp.ones(v.shape, BF16)], axis=1)
    got = jnp.dot(p, v, preferred_element_type=F32)
    if state is not None:
        got = got + state[1] * spread(jnp.exp2((state[0] - top) * EXP2_SCALE), 2 * DH)
    return top, got


def load_state(refs, t, lanes):
    o, l, m = (ref[t, :, lanes] for ref in refs)
    return m, jnp.concatenate([o, l], axis=1)


def save_state(refs, t, lanes, state):
    refs[0][t, :, lanes] = state[1][:, :DH]
    refs[1][t, :, lanes] = state[1][:, DH:]
    refs[2][t, :, lanes] = state[0]


def finish(state):
    top, got = state
    return jnp.where(top > 0.5 * NEG, got[:, :DH] / jnp.maximum(got[:, DH:], 1.0), 0.0)


def tiles(q_refs):
    for h in range(HEADS):
        lanes = slice(h * DH, (h + 1) * DH)
        for t in range(2):
            yield h // 4, lanes, t, q_refs[t][:, lanes]


def row_of(t, core, shape):
    return lax.broadcasted_iota(jnp.int32, shape, 0) + (core if t == 0 else 1 - core) * TOK


def own_kernel(qa_ref, qb_ref, kv_ref, *state_refs):
    core = where_am_i()[2]
    for pair, lanes, t, q in tiles((qa_ref, qb_ref)):

        def causal(s, t=t):
            col = lax.broadcasted_iota(jnp.int32, s.shape, 1)
            return jnp.where(col <= row_of(t, core, s.shape), s, NEG)

        at = slice(pair * DH, (pair + 1) * DH)
        save_state(state_refs, t, lanes, step(q, kv_ref[0, :, at], kv_ref[1, :, at], causal, None))


def prev_kernel(qa_ref, qb_ref, kv_ref, o_in, l_in, m_in, sum_ref, keep_ref, send_ref):
    row, chip, core = where_am_i()
    hidden = jnp.where(row + chip > 0, 0.0, NEG)
    for pair, lanes, t, q in tiles((qa_ref, qb_ref)):
        at = slice(pair * DH, (pair + 1) * DH)
        state = load_state((o_in, l_in, m_in), t, lanes)
        near = finish(step(q, kv_ref[0, :, at], kv_ref[1, :, at], lambda s: s + hidden, state))
        (keep_ref, send_ref)[t][:, lanes] = (near + sum_ref[t, :, lanes]).astype(BF16)


def mid_kernel(qa_ref, qb_ref, line_ref, up_ref, down_ref, far_up_ref, far_down_ref, tab_ref, out_ref, all_ref):
    core = where_am_i()[2]
    ends = tab_ref[2:3, :CHIP]

    def gather(*runs):
        at = 0
        for ref, start, n in runs:
            all_ref[at : at + n] = ref[start : start + n]
            at += n

    @pl.when(core == 0)
    def _():
        gather((line_ref, N_FAR, 4), (up_ref, 0, 4), (down_ref, N_FAR // 2, 4), (far_up_ref, 0, 4))

    @pl.when(core != 0)
    def _():
        gather((line_ref, N_FAR, 8), (far_up_ref, 0, 4), (far_down_ref, N_FAR // 2, 4))

    for pair, lanes, t, q in tiles((qa_ref, qb_ref)):

        def ended(s, t=t):
            return jnp.where(ends <= row_of(t, core, s.shape).astype(F32), s, NEG)

        k, v = (all_ref[:, pair, i].reshape(-1, DH) for i in range(2))
        out_ref[t, :, lanes] = finish(step(q, k, v, ended, None))


def far_kernel(steps, n_refs, first, last, *refs):
    qa_ref, qb_ref, tab_ref = refs[:3]
    part_refs, refs = refs[3 : 3 + n_refs], refs[3 + n_refs :]
    state_refs, refs = ([], refs) if first else (refs[:3], refs[3:])

    def run(chosen):
        for pair, lanes, t, q in tiles((qa_ref, qb_ref)):
            if not first:
                state = load_state(state_refs, t, lanes)
            else:
                state = None if chosen else (jnp.full((TOK, DH), NEG, F32), jnp.zeros((TOK, 2 * DH), F32))
            for i, start, n, row, lane in chosen:
                k, v = (part_refs[i][start : start + n, pair, j].reshape(-1, DH) for j in range(2))
                bias = tab_ref[row : row + 1, lane : lane + n * PIECE]
                state = step(q, k, v, lambda s, bias=bias: s + bias, state)
            if last:
                sum_ref, out_ref = refs
                out_ref[t, :, lanes] = finish(state) + sum_ref[t, :, lanes]
            else:
                save_state(refs, t, lanes, state)

    row, _, core = where_am_i()
    x_lo, z = row // N_Z, row % N_Z
    low, both = jnp.where(z > 0, 1, 0), jnp.where(x_lo > 0, 2, jnp.where(row > 0, 1, 0))
    mode = jnp.where(core == 0, both, 2 * low if steps[0][3] == 0 else 2 * x_lo)
    for which, chosen in enumerate(([], [each for each in steps if each[4] == 0], steps)):

        @pl.when(mode == which)
        def _(chosen=chosen):
            run(chosen)


def call(kernel, name, keys, out_shape, *args, scratch=()):
    rows = CHIP * HEADS
    return pl.pallas_call(
        kernel,
        in_specs=[VMEM] * len(args),
        out_specs=[VMEM] * len(out_shape),
        out_shape=out_shape,
        scratch_shapes=scratch,
        name=name,
        compiler_params=pltpu.CompilerParams(vmem_limit_bytes=24 << 20),
        cost_estimate=pl.CostEstimate(
            flops=6 * rows * keys * DH, bytes_accessed=6 << 20, transcendentals=rows * keys
        ),
    )(*args)


def far_call(name, steps, q_own, q_got, tab, parts, *more, first=False, last=False):
    kernel = functools.partial(far_kernel, steps, len(parts), first, last)
    keys = PIECE * sum(n for _, _, n, _, _ in steps)
    return call(kernel, name, keys, STATE[:1] if last else STATE, q_own, q_got, tab, *parts, *more)


def after(v, others):
    v, others = lax.optimization_barrier((v, others))
    return v, others


def body(queries, keys, values, *weights):
    kv_send, q_send, kv_own, q_own, *weights, tab = pack(queries, keys, values, *weights)
    chip_kv, mid, far = squeeze(kv_own, other_core(kv_send), *weights)
    q_send, far = after(q_send, far)
    q_got = other_core(q_send)

    near = call(own_kernel, "near_own", 512, STATE, q_own, q_got, chip_kv)
    got, near = after(hop(far, Z, 4), near)
    far = join([far, got], [(0, 0, 1), (1, 0, 1)])
    got = [hop(far, Z, d) for d in (1, -1, 2)]
    far = join([far, *got, mid], [(0, 0, 2), (1, 0, 2), (2, 0, 2), (3, 0, 2), (4, 0, N_MID)])
    got = [plane_hop(far, X, d) for d in (1, -1, 2)]
    line, up_a, down_a, up_b, down_b = lay_line(far, *[plane_hop(far, X, d) for d in (1, -1, 2)])
    up_a, down_a = plane_hop(up_a, Y, 1, True), plane_hop(down_a, Y, -1, True)
    up_b, down_b = plane_hop(up_b, Y, 1, True), plane_hop(down_b, Y, -1, True)
    state = far_call("far_0", [(0, 0, 16, 0, 0), (0, 16, 16, 0, 512)], q_own, q_got, tab, [line], first=True)
    (up_a, down_a), state = after((up_a, down_a), state)
    far_up, far_down = plane_hop(up_a, Y, 1, True), plane_hop(down_a, Y, -1, True)
    state = far_call("far_a", [(0, 4, 16, 1, 0), (1, 0, 16, 1, 512)], q_own, q_got, tab, [up_a, down_a], *state)
    (up_b, down_b), state = after((up_b, down_b), state)
    chip_kv, state = after(chip_kv, state)
    prev_kv = next_chip(chip_kv)
    state = far_call("far_b", [(0, 0, 16, 1, 512), (1, 0, 16, 1, 0)], q_own, q_got, tab, [up_b, down_b], *state)
    (total,) = call(
        mid_kernel, "mid", 512, STATE[:1], q_own, q_got, line, up_a, down_a, far_up, far_down, tab,
        scratch=[pltpu.VMEM(pieces(8 * N_MID).shape, BF16)],
    )
    (total,) = far_call(
        "far_2", [(0, 4, 16, 0, 0), (1, 0, 16, 0, 512)], q_own, q_got, tab, [far_up, far_down], *state, total, last=True
    )
    keep, send = call(prev_kernel, "near_prev", 512, [HALF] * 2, q_own, q_got, prev_kv, *near, total)
    return unpack(keep, other_core(send))


def solution(mesh):
    split = P(("row", "col"), None)
    return jax.shard_map(
        body,
        mesh=mesh,
        in_specs=(split, split, split, P(), P(), P(), P()),
        out_specs=split,
        check_vma=False,
    )
```
